512 devices in a mesh: ctx: 64 (over y_hi, z, core), ch: 8 (over y_lo, x).
Axes of the slice: x: 4, y: 8 (y_hi: 4, y_lo: 2; y = y_hi * 2 + y_lo), z: 8, core: 2. Of those that a mesh axis runs over, the one named last changes fastest.
Arguments:
- query_proj: bfloat16 [8192, 4096], P('ctx', 'ch'), may hold values from -6 to 6
- key_proj: bfloat16 [8192, 4096], P('ctx', 'ch'), may hold values from -6 to 6
- value_proj: bfloat16 [8192, 4096], P('ctx', 'ch'), may hold values from -6 to 6
- output_grad: bfloat16 [8192, 4096], P('ctx', 'ch'), may hold values from -6 to 6
- residue: float32 [4096, 16], P(('ch', 'ctx')), may hold values from -5 to 5
- decay_rate: float32 [4096, 16], P(('ch', 'ctx')), may hold values from 1.2207031e-05 to 0.0625
Outputs:
- query_grad: bfloat16 [8192, 4096], P('ctx', 'ch')
- key_grad: bfloat16 [8192, 4096], P('ctx', 'ch')
- value_grad: bfloat16 [8192, 4096], P('ctx', 'ch')
- residue_grad: float32 [4096, 16], P(('ch', 'ctx'))
- log_rate_grad: float32 [4096, 16], P(('ch', 'ctx'))
The draws below stay inside these ranges and needn't reach their ends.
All inputs are finite; a program needn't handle non-finite values.
Results may differ from the reference program's by a relative error of at most 0.0085.
Values may be sent and summed in bfloat16 or wider, within the bound.
A program may use at most 64 MiB of HBM per device.

```python
import math
import jax
import jax.numpy as jnp
from jax import lax

C = 4096
MODES = 16
TOKENS = 8192


def shard_levels(key, extent, pieces, smallest, top_value):
    def one(position, blocks):
        draws = jax.random.uniform(jax.random.fold_in(jax.random.fold_in(key, 6), position), (blocks,), jnp.float32, smallest / len(pieces), top_value / len(pieces))
        return jnp.repeat(jnp.exp(draws), extent[position] // blocks).reshape((-1,) + (1,) * (len(extent) - position - 1))

    gain = one(*pieces[0])
    for cut in pieces[1:]:
        gain = gain * one(*cut)
    return gain


def centred(stream_key, dims, scale, bound, cuts=(), kind=jnp.bfloat16):
    result = scale * jax.random.normal(stream_key, dims, jnp.float32)
    if cuts:
        result = result * shard_levels(stream_key, dims, cuts, -0.22, 0.18)
    return jnp.clip(result, -bound, bound).astype(kind)


def setup_inputs(seed: int = 0) -> dict:
    splits = jax.random.split(jax.random.key(seed), 7)
    query_proj = centred(splits[0], (TOKENS, C), 1.0, 6.0, ((0, 64), (1, 8)))
    key_proj = centred(splits[1], (TOKENS, C), 1.0, 6.0, ((0, 64), (1, 8)))
    value_proj = centred(splits[2], (TOKENS, C), 1.0, 6.0, ((0, 64), (1, 8)))
    output_grad = centred(splits[3], (TOKENS, C), 1.0, 6.0, ((0, 64), (1, 8)))
    residue = centred(splits[4], (C, MODES), 0.35, 5.0, ((0, 512),), jnp.float32)
    decay_rate = jnp.clip(jnp.exp(math.log(0.0625) - 8.54091 * jax.random.uniform(splits[5], (C, MODES), jnp.float32) ** shard_levels(splits[5], (C, MODES), ((0, 512),), -0.2, 0.2)), 1.220703143189894e-05, 0.0625)
    return dict(query_proj=query_proj, key_proj=key_proj, value_proj=value_proj, output_grad=output_grad, residue=residue, decay_rate=decay_rate)


def filter_bank(residue, decay_rate):
    positions = jnp.arange(TOKENS, dtype=jnp.float32)[None, :]
    filters = jnp.zeros((residue.shape[0], TOKENS), jnp.float32)
    for mode_index in range(MODES):
        rate = decay_rate[:, mode_index:mode_index + 1]
        filters = filters + residue[:, mode_index:mode_index + 1] * (jnp.sqrt(rate) * jnp.exp(-rate * positions))
    return filters

def parameter_grads(lag_grad, residue, decay_rate):
    positions = jnp.arange(TOKENS, dtype=jnp.float32)[None, :]
    residue_cols = []
    log_cols = []
    for mode_index in range(MODES):
        rate = decay_rate[:, mode_index:mode_index + 1]
        basis = jnp.sqrt(rate) * jnp.exp(-rate * positions)
        residue_cols.append(lax.optimization_barrier(jnp.sum(lag_grad * basis, axis=1)))
        log_cols.append(lax.optimization_barrier(jnp.sum(lag_grad * basis * (0.5 - rate * positions), axis=1)) * residue[:, mode_index])
    return (jnp.stack(residue_cols, axis=1), jnp.stack(log_cols, axis=1))

def reference(query_proj, key_proj, value_proj, output_grad, residue, decay_rate):
    length = 2 * TOKENS
    block_width = min(C, 256)
    blocks = C // block_width

    def regroup(whole):
        return whole.reshape(TOKENS, blocks, block_width).transpose(1, 0, 2)

    def one_block(block):
        query_rows, key_rows, value_rows, upstream, residue_rows, rate_rows = block
        filters = filter_bank(residue_rows, rate_rows)
        filter_spec = jnp.fft.rfft(filters, n=length, axis=1)
        gated = (key_rows.astype(jnp.float32) * value_rows.astype(jnp.float32)).astype(jnp.bfloat16)
        gate_grad = (upstream.astype(jnp.float32) * query_rows.astype(jnp.float32)).astype(jnp.bfloat16)
        gate_spec = jnp.fft.rfft(gated.astype(jnp.float32).T, n=length, axis=1)
        grad_spec = jnp.fft.rfft(gate_grad.astype(jnp.float32).T, n=length, axis=1)
        conv_out = jnp.fft.irfft(filter_spec * gate_spec, n=length, axis=1)[:, :TOKENS].astype(jnp.bfloat16).T
        conv_grad = jnp.fft.irfft(jnp.conj(filter_spec) * grad_spec, n=length, axis=1)[:, :TOKENS].astype(jnp.bfloat16).T
        lag_grad = jnp.fft.irfft(jnp.conj(gate_spec) * grad_spec, n=length, axis=1)[:, :TOKENS]
        query_grad = (upstream.astype(jnp.float32) * conv_out.astype(jnp.float32)).astype(jnp.bfloat16)
        key_grad = (conv_grad.astype(jnp.float32) * value_rows.astype(jnp.float32)).astype(jnp.bfloat16)
        value_grad = (conv_grad.astype(jnp.float32) * key_rows.astype(jnp.float32)).astype(jnp.bfloat16)
        residue_grad, log_rate_grad = parameter_grads(lag_grad, residue_rows, rate_rows)
        return (query_grad, key_grad, value_grad, residue_grad, log_rate_grad)
    outs = lax.map(one_block, (regroup(query_proj), regroup(key_proj), regroup(value_proj), regroup(output_grad), residue.reshape(blocks, block_width, MODES), decay_rate.reshape(blocks, block_width, MODES)))

    def ungroup(parts):
        return parts.transpose(1, 0, 2).reshape(TOKENS, C)
    scale = TOKENS ** (-0.5)
    return (ungroup(outs[0]), ungroup(outs[1]), ungroup(outs[2]), outs[3].reshape(C, MODES) * scale, outs[4].reshape(C, MODES) * scale)
```

```python
import functools
import math

import jax
import jax.numpy as jnp
from jax import lax
from jax.experimental import pallas as pl
from jax.experimental.pallas import tpu as pltpu
from jax.sharding import PartitionSpec as P

MESH = pl.DeviceIdType.MESH
F32 = jnp.float32
BF16 = jnp.bfloat16
HIGHEST = lax.Precision.HIGHEST
BLOCK = 128
OWN = 8
LANES = 128


def dot(left, right, dims=((1,), (0,)), precision=None):
    return lax.dot_general(
        left, right, (dims, ((), ())), precision=precision, preferred_element_type=F32
    )


def split(value):
    high = value.astype(BF16)
    return high, (value - high.astype(F32)).astype(BF16)


def iota(shape, axis):
    return lax.broadcasted_iota(jnp.int32, shape, axis)


def shift_rows(value, step, down):
    rows = value.shape[0]
    index = iota(value.shape, 0)
    if down:
        return jnp.where(index >= step, pltpu.roll(value, step, 0), 0.0)
    return jnp.where(index < rows - step, pltpu.roll(value, rows - step, 0), 0.0)


def scan_blocks(state, rate_row, down):
    step = 1
    while step < state.shape[0]:
        decay = jnp.exp(rate_row * (-float(BLOCK * step)))
        state = state + decay * shift_rows(state, step, down)
        step *= 2
    return shift_rows(state, 1, down)


def scan_moments(state, moment, rate_row):
    step = 1
    while step < state.shape[0]:
        decay = jnp.exp(rate_row * (-float(BLOCK * step)))
        below = shift_rows(state, step, True)
        moment = moment + decay * (
            shift_rows(moment, step, True) + float(BLOCK * step) * below
        )
        state = state + decay * below
        step *= 2
    return shift_rows(state, 1, True), shift_rows(moment, 1, True)


def own_rows(stacked, blocks):
    group = iota((blocks, LANES), 1) // 16
    total = jnp.zeros((blocks, LANES), F32)
    for channel in range(OWN):
        part = stacked[channel * blocks : (channel + 1) * blocks]
        total = jnp.where(group == channel, part, total)
    return total


def kernel(
    sizes,
    scale,
    query_ref,
    key_ref,
    value_ref,
    upstream_ref,
    residue_ref,
    rate_ref,
    out_ref,
    grad_ref,
    residue_grad_ref,
    rate_grad_ref,
    query_in,
    key_in,
    value_in,
    upstream_in,
    send_a,
    recv_a,
    send_b,
    recv_b,
    wide,
    xs,
    gs,
    toep_hi,
    toep_lo,
    tables,
    in_sems,
    send_sems,
    recv_sems,
):
    blocks_y, blocks_z = sizes
    blocks = blocks_y * blocks_z * 2
    me = lax.axis_index("ctx")
    my_core = lax.rem(me, 2)
    my_z = lax.rem(me // 2, blocks_z)
    my_y = me // (2 * blocks_z)

    def peer_of(step):
        step_z = lax.rem(step, blocks_z)
        rest = step // blocks_z
        step_core = lax.rem(rest, 2)
        step_y = rest // 2
        half_z = (step_z + 1) // 2
        delta_z = blocks_z // 2 + (1 - 2 * lax.rem(step_z, 2)) * half_z + blocks_z
        delta_y = blocks_y - 1 - step_y
        z = lax.rem(my_z + delta_z, blocks_z)
        y = lax.rem(my_y + delta_y, blocks_y)
        core = lax.rem(my_core + 1 + step_core, 2)
        return (y * blocks_z + z) * 2 + core

    barrier = pltpu.get_barrier_semaphore()

    def greet(step, carry):
        pl.semaphore_signal(
            barrier, inc=1, device_id={"ctx": peer_of(step)}, device_id_type=MESH
        )
        return carry

    lax.fori_loop(0, blocks - 1, greet, 0)

    loads = []
    for place, (source, target) in enumerate(
        ((key_ref, key_in), (value_ref, value_in), (query_ref, query_in), (upstream_ref, upstream_in))
    ):
        load = pltpu.make_async_copy(source, target, in_sems.at[place])
        load.start()
        loads.append(load)

    rate = rate_ref[...]
    residue = residue_ref[...]
    spread = (iota((16, LANES), 1) % 16 == iota((16, LANES), 0)).astype(F32)
    own_lane = iota((OWN, LANES), 1) // 16 == iota((OWN, LANES), 0)

    def to_row(params):
        tiled = dot(params, spread, precision=HIGHEST)
        return jnp.sum(jnp.where(own_lane, tiled, 0.0), axis=0, keepdims=True)

    rate_row = to_row(rate)
    gain_row = to_row(residue * jnp.sqrt(rate))

    for load in loads:
        load.wait()
    channels = blocks * OWN
    for first in range(0, channels, LANES):
        cols = pl.ds(first, LANES)
        gated = (key_in[:, cols].astype(F32) * value_in[:, cols].astype(F32)).astype(BF16)
        gate_grad = (upstream_in[:, cols].astype(F32) * query_in[:, cols].astype(F32)).astype(BF16)
        gated = jnp.transpose(gated.astype(F32)).reshape(LANES // OWN, OWN, BLOCK)
        gate_grad = jnp.transpose(gate_grad.astype(F32)).reshape(LANES // OWN, OWN, BLOCK)
        send_a[pl.ds(first // OWN, LANES // OWN)] = jnp.concatenate(
            [gated, gate_grad], axis=1
        ).astype(BF16)

    pl.semaphore_wait(barrier, blocks - 1)

    def exchange(send, recv, phase):
        def push(step, carry):
            peer = peer_of(step)
            pltpu.make_async_remote_copy(
                src_ref=send.at[peer],
                dst_ref=recv.at[me],
                send_sem=send_sems.at[phase],
                recv_sem=recv_sems.at[phase],
                device_id={"ctx": peer},
                device_id_type=MESH,
            ).start()
            return carry

        lax.fori_loop(0, blocks - 1, push, 0)
        pltpu.make_async_copy(send.at[me], recv.at[me], recv_sems.at[phase]).start()

    def arrived(recv, phase):
        pltpu.make_async_copy(recv, recv, recv_sems.at[phase]).wait()

    def sent(send, phase):
        rest = send.at[pl.ds(0, blocks - 1)]
        pltpu.make_async_copy(rest, rest, send_sems.at[phase]).wait()

    exchange(send_a, recv_a, 0)

    place_row = iota((BLOCK, LANES), 0).astype(F32)
    place_lane = iota((OWN, LANES), 1).astype(F32)
    ahead = jnp.exp(-rate_row * (float(BLOCK - 1) - place_row))
    behind = jnp.exp(-rate_row * (place_row + 1.0))
    for place, table in enumerate((ahead, behind, gain_row * behind, gain_row * ahead)):
        high, low = split(table)
        tables[2 * place] = high
        tables[2 * place + 1] = low
    taps = jnp.zeros((OWN, LANES), F32)
    for mode in range(16):
        mode_rate = rate[:, mode : mode + 1]
        taps = taps + residue[:, mode : mode + 1] * (
            jnp.sqrt(mode_rate) * jnp.exp(-mode_rate * place_lane)
        )
    causal = iota((BLOCK, BLOCK), 1) >= iota((BLOCK, BLOCK), 0)
    for channel in range(OWN):
        row = jnp.broadcast_to(taps[channel : channel + 1], (BLOCK, LANES))
        row = pltpu.roll(row, 0, 1, stride=1, stride_axis=0)
        high, low = split(jnp.where(causal, row, 0.0))
        toep_hi[channel] = high
        toep_lo[channel] = low

    arrived(recv_a, 0)
    wide[...] = recv_a[...].astype(F32).reshape(blocks * 16, BLOCK)
    for channel in range(OWN):
        rows = pl.ds(channel * blocks, blocks)
        xs[rows, :] = wide[pl.ds(channel, blocks, stride=16), :].astype(BF16)
        gs[rows, :] = wide[pl.ds(OWN + channel, blocks, stride=16), :].astype(BF16)
    x_all = xs[...]
    g_all = gs[...]
    x_ends = own_rows(dot(x_all, tables[0]) + dot(x_all, tables[1]), blocks)
    g_ends = own_rows(dot(g_all, tables[2]) + dot(g_all, tables[3]), blocks)
    x_state = scan_blocks(x_ends, rate_row, True)
    g_state = scan_blocks(g_ends, rate_row, False)
    group = iota((blocks, LANES), 1) // 16

    def carried(state, high, low):
        parts = jnp.concatenate(
            [jnp.where(group == channel, state, 0.0) for channel in range(OWN)], axis=0
        )
        part_hi, part_lo = split(parts)
        over = ((1,), (1,))
        return dot(part_hi, high, over) + dot(part_lo, high, over) + dot(part_hi, low, over)

    x_carried = carried(x_state, tables[4], tables[5])
    g_carried = carried(g_state, tables[6], tables[7])
    for channel in range(OWN):
        rows = slice(channel * blocks, (channel + 1) * blocks)
        x_own = x_all[rows]
        g_own = g_all[rows]
        high = toep_hi[channel]
        low = toep_lo[channel]
        over = ((1,), (1,))
        wide[pl.ds(channel, blocks, stride=16), :] = (
            dot(x_own, high) + dot(x_own, low) + x_carried[rows]
        )
        wide[pl.ds(OWN + channel, blocks, stride=16), :] = (
            dot(g_own, high, over) + dot(g_own, low, over) + g_carried[rows]
        )
    send_b[...] = wide[...].reshape(blocks, 16, BLOCK).astype(BF16)
    exchange(send_b, recv_b, 1)

    high, low = split(ahead * (float(BLOCK - 1) - place_row))
    x_slopes = own_rows(dot(x_all, high) + dot(x_all, low), blocks)
    high, low = split(behind * (place_row + 1.0))
    g_slopes = own_rows(dot(g_all, high) + dot(g_all, low), blocks)
    x_state, x_moment = scan_moments(x_ends, x_slopes, rate_row)
    plain = jnp.sum(g_ends * x_state, axis=0, keepdims=True)
    sloped = jnp.sum(g_ends * x_moment + g_slopes * x_state, axis=0, keepdims=True)
    reverse = (iota((BLOCK, BLOCK), 0) + iota((BLOCK, BLOCK), 1) == BLOCK - 1).astype(BF16)
    x_reversed = dot(x_all, reverse).astype(BF16)
    paired = iota((BLOCK, BLOCK), 0) + iota((BLOCK, BLOCK), 1) >= BLOCK - 1
    lags = []
    for channel in range(OWN):
        rows = slice(channel * blocks, (channel + 1) * blocks)
        pairs = dot(g_all[rows], x_reversed[rows], ((0,), (0,)))
        pairs = jnp.where(paired, pairs, 0.0)
        pairs = pltpu.roll(pairs, 1, 1, stride=1, stride_axis=0)
        lags.append(jnp.sum(pairs, axis=0, keepdims=True))
    lags = jnp.concatenate(lags, axis=0)
    decays = jnp.exp(-rate_row * place_row)

    def own_sum(table):
        full = dot(lags, table, precision=HIGHEST)
        return jnp.sum(jnp.where(own_lane, full, 0.0), axis=0, keepdims=True)

    plain = plain + own_sum(decays)
    sloped = sloped + own_sum(decays * place_row)
    root_row = jnp.sqrt(rate_row) * scale
    residue_row = to_row(residue)
    gather = (iota((LANES, 16), 0) % 16 == iota((LANES, 16), 1)).astype(F32)

    def from_row(row):
        rows = jnp.where(own_lane, jnp.broadcast_to(row, (OWN, LANES)), 0.0)
        return dot(rows, gather, precision=HIGHEST)

    residue_grad_ref[...] = from_row(root_row * plain)
    rate_grad_ref[...] = from_row(root_row * residue_row * (0.5 * plain - rate_row * sloped))

    arrived(recv_b, 1)
    for first in range(0, channels, LANES):
        cols = pl.ds(first, LANES)
        both = recv_b[pl.ds(first // OWN, LANES // OWN)].astype(F32)
        out_ref[:, cols] = jnp.transpose(both[:, :OWN].reshape(LANES, BLOCK)).astype(BF16)
        grad_ref[:, cols] = jnp.transpose(both[:, OWN:].reshape(LANES, BLOCK)).astype(BF16)
    sent(send_a, 0)
    sent(send_b, 1)


def times_bf16(left, right):
    return (left.astype(F32) * right.astype(F32)).astype(BF16)


def local(sizes, query_proj, key_proj, value_proj, output_grad, residue, decay_rate):
    tok_dev, channels = query_proj.shape
    blocks = sizes[0] * sizes[1] * 2
    scale = float(tok_dev * blocks) ** (-0.5)
    anywhere = pl.BlockSpec(memory_space=pl.ANY)
    vmem = pl.BlockSpec(memory_space=pltpu.VMEM)
    tokens = jax.ShapeDtypeStruct((tok_dev, channels), BF16)
    params = jax.ShapeDtypeStruct(residue.shape, F32)
    message = pltpu.VMEM((blocks, 16, BLOCK), BF16)
    conv_out, conv_grad, residue_grad, rate_grad = pl.pallas_call(
        functools.partial(kernel, sizes, scale),
        out_shape=(tokens, tokens, params, params),
        in_specs=[anywhere] * 4 + [vmem] * 2,
        out_specs=[vmem] * 4,
        scratch_shapes=[pltpu.VMEM((tok_dev, channels), BF16)] * 4
        + [message] * 4
        + [
            pltpu.VMEM((blocks * 16, BLOCK), F32),
            pltpu.VMEM((blocks * OWN, BLOCK), BF16),
            pltpu.VMEM((blocks * OWN, BLOCK), BF16),
            pltpu.VMEM((OWN, BLOCK, BLOCK), BF16),
            pltpu.VMEM((OWN, BLOCK, BLOCK), BF16),
            pltpu.VMEM((8, BLOCK, LANES), BF16),
            pltpu.SemaphoreType.DMA((4,)),
            pltpu.SemaphoreType.DMA((2,)),
            pltpu.SemaphoreType.DMA((2,)),
        ],
        compiler_params=pltpu.CompilerParams(collective_id=0, has_side_effects=True),
    )(query_proj, key_proj, value_proj, output_grad, residue, decay_rate)
    query_grad = times_bf16(output_grad, conv_out)
    key_grad = times_bf16(conv_grad, value_proj)
    value_grad = times_bf16(conv_grad, key_proj)
    return query_grad, key_grad, value_grad, residue_grad, rate_grad


def solution(mesh):
    ranks = mesh.shape["ctx"]
    along_z = min(8, ranks // 2)
    sizes = (ranks // (2 * along_z), along_z)
    tokens = P("ctx", "ch")
    params = P(("ch", "ctx"), None)
    return jax.shard_map(
        functools.partial(local, sizes),
        mesh=mesh,
        in_specs=(tokens,) * 4 + (params,) * 2,
        out_specs=(tokens,) * 3 + (params,) * 2,
        check_vma=False,
    )
```

```python
import functools
import math

import jax
import jax.numpy as jnp
from jax import lax
from jax.experimental import pallas as pl
from jax.experimental.pallas import tpu as pltpu
from jax.sharding import PartitionSpec as P

MESH = pl.DeviceIdType.MESH
F32 = jnp.float32
BF16 = jnp.bfloat16
HIGHEST = lax.Precision.HIGHEST
BLOCK = 128
OWN = 8
LANES = 128


def dot(left, right, dims=((1,), (0,)), precision=None):
    return lax.dot_general(
        left, right, (dims, ((), ())), precision=precision, preferred_element_type=F32
    )


def split(value):
    high = value.astype(BF16)
    return high, (value - high.astype(F32)).astype(BF16)


def iota(shape, axis):
    return lax.broadcasted_iota(jnp.int32, shape, axis)


def shift_rows(value, step, down):
    rows = value.shape[0]
    index = iota(value.shape, 0)
    if down:
        return jnp.where(index >= step, pltpu.roll(value, step, 0), 0.0)
    return jnp.where(index < rows - step, pltpu.roll(value, rows - step, 0), 0.0)


def scan_blocks(state, rate_row, down):
    step = 1
    while step < state.shape[0]:
        decay = jnp.exp(rate_row * (-float(BLOCK * step)))
        state = state + decay * shift_rows(state, step, down)
        step *= 2
    return shift_rows(state, 1, down)


def scan_moments(state, moment, rate_row):
    step = 1
    while step < state.shape[0]:
        decay = jnp.exp(rate_row * (-float(BLOCK * step)))
        below = shift_rows(state, step, True)
        moment = moment + decay * (
            shift_rows(moment, step, True) + float(BLOCK * step) * below
        )
        state = state + decay * below
        step *= 2
    return shift_rows(state, 1, True), shift_rows(moment, 1, True)


def own_rows(stacked, blocks):
    group = iota((blocks, LANES), 1) // 16
    total = jnp.zeros((blocks, LANES), F32)
    for channel in range(OWN):
        part = stacked[channel * blocks : (channel + 1) * blocks]
        total = jnp.where(group == channel, part, total)
    return total


def kernel(
    sizes,
    scale,
    query_ref,
    key_ref,
    value_ref,
    upstream_ref,
    residue_ref,
    rate_ref,
    out_ref,
    grad_ref,
    residue_grad_ref,
    rate_grad_ref,
    query_in,
    key_in,
    value_in,
    upstream_in,
    send_a,
    recv_a,
    send_b,
    recv_b,
    wide,
    xs,
    gs,
    toep_hi,
    toep_lo,
    tables,
    in_sems,
    send_sems,
    recv_sems,
):
    blocks_y, blocks_z = sizes
    blocks = blocks_y * blocks_z * 2
    me = lax.axis_index("ctx")
    my_core = lax.rem(me, 2)
    my_z = lax.rem(me // 2, blocks_z)
    my_y = me // (2 * blocks_z)

    def peer_of(step):
        step_z = lax.rem(step, blocks_z)
        rest = step // blocks_z
        step_core = lax.rem(rest, 2)
        step_y = rest // 2
        half_z = (step_z + 1) // 2
        delta_z = blocks_z // 2 + (1 - 2 * lax.rem(step_z, 2)) * half_z + blocks_z
        delta_y = blocks_y - 1 - step_y
        z = lax.rem(my_z + delta_z, blocks_z)
        y = lax.rem(my_y + delta_y, blocks_y)
        core = lax.rem(my_core + 1 + step_core, 2)
        return (y * blocks_z + z) * 2 + core

    barrier = pltpu.get_barrier_semaphore()

    def greet(step, carry):
        pl.semaphore_signal(
            barrier, inc=1, device_id={"ctx": peer_of(step)}, device_id_type=MESH
        )
        return carry

    lax.fori_loop(0, blocks - 1, greet, 0)

    loads = []
    for place, (source, target) in enumerate(
        ((key_ref, key_in), (value_ref, value_in), (query_ref, query_in), (upstream_ref, upstream_in))
    ):
        load = pltpu.make_async_copy(source, target, in_sems.at[place])
        load.start()
        loads.append(load)

    rate = rate_ref[...]
    residue = residue_ref[...]
    spread = (iota((16, LANES), 1) % 16 == iota((16, LANES), 0)).astype(F32)
    own_lane = iota((OWN, LANES), 1) // 16 == iota((OWN, LANES), 0)

    def to_row(params):
        tiled = dot(params, spread, precision=HIGHEST)
        return jnp.sum(jnp.where(own_lane, tiled, 0.0), axis=0, keepdims=True)

    rate_row = to_row(rate)
    gain_row = to_row(residue * jnp.sqrt(rate))

    for load in loads:
        load.wait()
    channels = blocks * OWN
    for first in range(0, channels, LANES):
        cols = pl.ds(first, LANES)
        gated = (key_in[:, cols].astype(F32) * value_in[:, cols].astype(F32)).astype(BF16)
        gate_grad = (upstream_in[:, cols].astype(F32) * query_in[:, cols].astype(F32)).astype(BF16)
        gated = jnp.transpose(gated.astype(F32)).reshape(LANES // OWN, OWN, BLOCK)
        gate_grad = jnp.transpose(gate_grad.astype(F32)).reshape(LANES // OWN, OWN, BLOCK)
        send_a[pl.ds(first // OWN, LANES // OWN)] = jnp.concatenate(
            [gated, gate_grad], axis=1
        ).astype(BF16)

    pl.semaphore_wait(barrier, blocks - 1)

    def exchange(send, recv, phase):
        def push(step, carry):
            peer = peer_of(step)
            pltpu.make_async_remote_copy(
                src_ref=send.at[peer],
                dst_ref=recv.at[me],
                send_sem=send_sems.at[phase],
                recv_sem=recv_sems.at[phase],
                device_id={"ctx": peer},
                device_id_type=MESH,
            ).start()
            return carry

        lax.fori_loop(0, blocks - 1, push, 0)
        pltpu.make_async_copy(send.at[me], recv.at[me], recv_sems.at[phase]).start()

    def arrived(recv, phase):
        pltpu.make_async_copy(recv, recv, recv_sems.at[phase]).wait()

    def sent(send, phase):
        rest = send.at[pl.ds(0, blocks - 1)]
        pltpu.make_async_copy(rest, rest, send_sems.at[phase]).wait()

    exchange(send_a, recv_a, 0)

    place_row = iota((BLOCK, LANES), 0).astype(F32)
    place_lane = iota((OWN, LANES), 1).astype(F32)
    ahead = jnp.exp(-rate_row * (float(BLOCK - 1) - place_row))
    behind = jnp.exp(-rate_row * (place_row + 1.0))
    for place, table in enumerate((ahead, behind, gain_row * behind, gain_row * ahead)):
        high, low = split(table)
        tables[2 * place] = high
        tables[2 * place + 1] = low
    taps = jnp.zeros((OWN, LANES), F32)
    for mode in range(16):
        mode_rate = rate[:, mode : mode + 1]
        taps = taps + residue[:, mode : mode + 1] * (
            jnp.sqrt(mode_rate) * jnp.exp(-mode_rate * place_lane)
        )
    causal = iota((BLOCK, BLOCK), 1) >= iota((BLOCK, BLOCK), 0)
    for channel in range(OWN):
        row = jnp.broadcast_to(taps[channel : channel + 1], (BLOCK, LANES))
        row = pltpu.roll(row, 0, 1, stride=1, stride_axis=0)
        high, low = split(jnp.where(causal, row, 0.0))
        toep_hi[channel] = high
        toep_lo[channel] = low

    arrived(recv_a, 0)
    wide[...] = recv_a[...].astype(F32).reshape(blocks * 16, BLOCK)
    for channel in range(OWN):
        rows = pl.ds(channel * blocks, blocks)
        xs[rows, :] = wide[pl.ds(channel, blocks, stride=16), :].astype(BF16)
        gs[rows, :] = wide[pl.ds(OWN + channel, blocks, stride=16), :].astype(BF16)
    x_all = xs[...]
    g_all = gs[...]
    x_ends = own_rows(dot(x_all, tables[0]) + dot(x_all, tables[1]), blocks)
    g_ends = own_rows(dot(g_all, tables[2]) + dot(g_all, tables[3]), blocks)
    x_state = scan_blocks(x_ends, rate_row, True)
    g_state = scan_blocks(g_ends, rate_row, False)
    group = iota((blocks, LANES), 1) // 16

    def carried(state, high, low):
        parts = jnp.concatenate(
            [jnp.where(group == channel, state, 0.0) for channel in range(OWN)], axis=0
        )
        part_hi, part_lo = split(parts)
        over = ((1,), (1,))
        return dot(part_hi, high, over) + dot(part_lo, high, over) + dot(part_hi, low, over)

    x_carried = carried(x_state, tables[4], tables[5])
    g_carried = carried(g_state, tables[6], tables[7])
    for channel in range(OWN):
        rows = slice(channel * blocks, (channel + 1) * blocks)
        x_own = x_all[rows]
        g_own = g_all[rows]
        high = toep_hi[channel]
        low = toep_lo[channel]
        over = ((1,), (1,))
        wide[pl.ds(channel, blocks, stride=16), :] = (
            dot(x_own, high) + dot(x_own, low) + x_carried[rows]
        )
        wide[pl.ds(OWN + channel, blocks, stride=16), :] = (
            dot(g_own, high, over) + dot(g_own, low, over) + g_carried[rows]
        )
    send_b[...] = wide[...].reshape(blocks, 16, BLOCK).astype(BF16)
    exchange(send_b, recv_b, 1)

    high, low = split(ahead * (float(BLOCK - 1) - place_row))
    x_slopes = own_rows(dot(x_all, high) + dot(x_all, low), blocks)
    high, low = split(behind * (place_row + 1.0))
    g_slopes = own_rows(dot(g_all, high) + dot(g_all, low), blocks)
    x_state, x_moment = scan_moments(x_ends, x_slopes, rate_row)
    plain = jnp.sum(g_ends * x_state, axis=0, keepdims=True)
    sloped = jnp.sum(g_ends * x_moment + g_slopes * x_state, axis=0, keepdims=True)
    reverse = (iota((BLOCK, BLOCK), 0) + iota((BLOCK, BLOCK), 1) == BLOCK - 1).astype(BF16)
    x_reversed = dot(x_all, reverse).astype(BF16)
    paired = iota((BLOCK, BLOCK), 0) + iota((BLOCK, BLOCK), 1) >= BLOCK - 1
    lags = []
    for channel in range(OWN):
        rows = slice(channel * blocks, (channel + 1) * blocks)
        pairs = dot(g_all[rows], x_reversed[rows], ((0,), (0,)))
        pairs = jnp.where(paired, pairs, 0.0)
        pairs = pltpu.roll(pairs, 1, 1, stride=1, stride_axis=0)
        lags.append(jnp.sum(pairs, axis=0, keepdims=True))
    lags = jnp.concatenate(lags, axis=0)
    decays = jnp.exp(-rate_row * place_row)

    def own_sum(table):
        full = dot(lags, table, precision=HIGHEST)
        return jnp.sum(jnp.where(own_lane, full, 0.0), axis=0, keepdims=True)

    plain = plain + own_sum(decays)
    sloped = sloped + own_sum(decays * place_row)
    root_row = jnp.sqrt(rate_row) * scale
    residue_row = to_row(residue)
    gather = (iota((LANES, 16), 0) % 16 == iota((LANES, 16), 1)).astype(F32)

    def from_row(row):
        rows = jnp.where(own_lane, jnp.broadcast_to(row, (OWN, LANES)), 0.0)
        return dot(rows, gather, precision=HIGHEST)

    residue_grad_ref[...] = from_row(root_row * plain)
    rate_grad_ref[...] = from_row(root_row * residue_row * (0.5 * plain - rate_row * sloped))

    arrived(recv_b, 1)
    for first in range(0, channels, LANES):
        cols = pl.ds(first, LANES)
        both = recv_b[pl.ds(first // OWN, LANES // OWN)].astype(F32)
        out_ref[:, cols] = jnp.transpose(both[:, :OWN].reshape(LANES, BLOCK)).astype(BF16)
        grad_ref[:, cols] = jnp.transpose(both[:, OWN:].reshape(LANES, BLOCK)).astype(BF16)
    sent(send_a, 0)
    sent(send_b, 1)


def finish(
    upstream_ref,
    value_ref,
    key_ref,
    out_ref,
    grad_ref,
    residue_grad_ref,
    rate_grad_ref,
    query_grad_hbm,
    key_grad_hbm,
    value_grad_hbm,
    residue_grad_hbm,
    rate_grad_hbm,
    query_grad,
    key_grad,
    value_grad,
    out_sems,
):
    stores = [
        pltpu.make_async_copy(source, target, out_sems.at[place])
        for place, (source, target) in enumerate(
            (
                (query_grad, query_grad_hbm),
                (key_grad, key_grad_hbm),
                (value_grad, value_grad_hbm),
                (residue_grad_ref, residue_grad_hbm),
                (rate_grad_ref, rate_grad_hbm),
            )
        )
    ]
    stores[3].start()
    stores[4].start()
    products = (
        (upstream_ref, out_ref, query_grad),
        (value_ref, grad_ref, key_grad),
        (key_ref, grad_ref, value_grad),
    )
    for store, (gate, result, target) in zip(stores, products):
        target[...] = (gate[...].astype(F32) * result[...].astype(F32)).astype(BF16)
        store.start()
    for store in stores:
        store.wait()


def local(sizes, query_proj, key_proj, value_proj, output_grad, residue, decay_rate):
    tok_dev, channels = query_proj.shape
    blocks = sizes[0] * sizes[1] * 2
    scale = float(tok_dev * blocks) ** (-0.5)
    anywhere = pl.BlockSpec(memory_space=pl.ANY)
    vmem = pl.BlockSpec(memory_space=pltpu.VMEM)
    tokens = jax.ShapeDtypeStruct((tok_dev, channels), BF16)
    params = jax.ShapeDtypeStruct(residue.shape, F32)
    message = pltpu.VMEM((blocks, 16, BLOCK), BF16)
    tokens_vmem = pltpu.VMEM(tokens.shape, BF16)
    params_vmem = pltpu.VMEM(params.shape, F32)
    conv_out, conv_grad, residue_grad, rate_grad = pl.pallas_call(
        functools.partial(kernel, sizes, scale),
        out_shape=(tokens_vmem, tokens_vmem, params_vmem, params_vmem),
        in_specs=[anywhere] * 4 + [vmem] * 2,
        out_specs=[vmem] * 4,
        scratch_shapes=[pltpu.VMEM((tok_dev, channels), BF16)] * 4
        + [message] * 4
        + [
            pltpu.VMEM((blocks * 16, BLOCK), F32),
            pltpu.VMEM((blocks * OWN, BLOCK), BF16),
            pltpu.VMEM((blocks * OWN, BLOCK), BF16),
            pltpu.VMEM((OWN, BLOCK, BLOCK), BF16),
            pltpu.VMEM((OWN, BLOCK, BLOCK), BF16),
            pltpu.VMEM((8, BLOCK, LANES), BF16),
            pltpu.SemaphoreType.DMA((4,)),
            pltpu.SemaphoreType.DMA((2,)),
            pltpu.SemaphoreType.DMA((2,)),
        ],
        compiler_params=pltpu.CompilerParams(collective_id=0, has_side_effects=True, vmem_limit_bytes=60 * 1024 * 1024),
    )(query_proj, key_proj, value_proj, output_grad, residue, decay_rate)
    return pl.pallas_call(
        finish,
        out_shape=(tokens,) * 3 + (params,) * 2,
        in_specs=[vmem] * 7,
        out_specs=[anywhere] * 5,
        scratch_shapes=[pltpu.VMEM((tok_dev, channels), BF16)] * 3
        + [pltpu.SemaphoreType.DMA((5,))],
        compiler_params=pltpu.CompilerParams(vmem_limit_bytes=8 << 20),
    )(output_grad, value_proj, key_proj, conv_out, conv_grad, residue_grad, rate_grad)


def solution(mesh):
    ranks = mesh.shape["ctx"]
    along_z = min(8, ranks // 2)
    sizes = (ranks // (2 * along_z), along_z)
    tokens = P("ctx", "ch")
    params = P(("ch", "ctx"), None)
    return jax.shard_map(
        functools.partial(local, sizes),
        mesh=mesh,
        in_specs=(tokens,) * 4 + (params,) * 2,
        out_specs=(tokens,) * 3 + (params,) * 2,
        check_vma=False,
    )
```

```python
import functools
import math

import jax
import jax.numpy as jnp
from jax import lax
from jax.experimental import pallas as pl
from jax.experimental.pallas import tpu as pltpu
from jax.sharding import PartitionSpec as P

MESH = pl.DeviceIdType.MESH
F32 = jnp.float32
BF16 = jnp.bfloat16
HIGHEST = lax.Precision.HIGHEST
BLOCK = 128
OWN = 8
LANES = 128


def dot(left, right, dims=((1,), (0,)), precision=None):
    return lax.dot_general(
        left, right, (dims, ((), ())), precision=precision, preferred_element_type=F32
    )


def split(value):
    high = value.astype(BF16)
    return high, (value - high.astype(F32)).astype(BF16)


def iota(shape, axis):
    return lax.broadcasted_iota(jnp.int32, shape, axis)


def shift_rows(value, step, down):
    rows = value.shape[0]
    index = iota(value.shape, 0)
    if down:
        return jnp.where(index >= step, pltpu.roll(value, step, 0), 0.0)
    return jnp.where(index < rows - step, pltpu.roll(value, rows - step, 0), 0.0)


def scan_blocks(state, rate_row, down):
    step = 1
    while step < state.shape[0]:
        decay = jnp.exp(rate_row * (-float(BLOCK * step)))
        state = state + decay * shift_rows(state, step, down)
        step *= 2
    return shift_rows(state, 1, down)


def scan_moments(state, moment, rate_row):
    step = 1
    while step < state.shape[0]:
        decay = jnp.exp(rate_row * (-float(BLOCK * step)))
        below = shift_rows(state, step, True)
        moment = moment + decay * (
            shift_rows(moment, step, True) + float(BLOCK * step) * below
        )
        state = state + decay * below
        step *= 2
    return shift_rows(state, 1, True), shift_rows(moment, 1, True)


def own_rows(stacked, blocks):
    group = iota((blocks, LANES), 1) // 16
    total = jnp.zeros((blocks, LANES), F32)
    for channel in range(OWN):
        part = stacked[channel * blocks : (channel + 1) * blocks]
        total = jnp.where(group == channel, part, total)
    return total


def kernel(
    sizes,
    scale,
    query_ref,
    key_ref,
    value_ref,
    upstream_ref,
    residue_ref,
    rate_ref,
    out_ref,
    grad_ref,
    residue_grad_ref,
    rate_grad_ref,
    query_in,
    key_in,
    value_in,
    upstream_in,
    send_a,
    recv_a,
    send_b,
    recv_b,
    wide,
    xs,
    gs,
    toep_hi,
    toep_lo,
    tables,
    in_sems,
    send_sems,
    recv_sems,
    ready_sem,
    relay_sem,
):
    blocks_y, blocks_z = sizes
    blocks = blocks_y * blocks_z * 2
    me = lax.axis_index("ctx")
    my_core = lax.rem(me, 2)
    my_z = lax.rem(me // 2, blocks_z)
    my_y = me // (2 * blocks_z)

    half = blocks_z // 2
    members = blocks // 2
    my_base = (my_z // half) * half
    is_first = my_z < half

    def peer_of(base, step):
        delta_z = lax.rem(step, half)
        rest = step // half
        z = base + lax.rem(lax.rem(my_z, half) + delta_z, half)
        y = lax.rem(my_y + rest // 2, blocks_y)
        core = lax.rem(my_core + rest, 2)
        return (y * blocks_z + z) * 2 + core

    def signal(semaphore, peer):
        pl.semaphore_signal(semaphore, inc=1, device_id={"ctx": peer}, device_id_type=MESH)

    def for_peers(base, action):
        def one(step, carry):
            action(peer_of(base, step))
            return carry

        lax.fori_loop(jnp.where(my_base == base, 1, 0), members, one, 0)

    barrier = pltpu.get_barrier_semaphore()

    @pl.when(is_first)
    def _():
        for_peers(0, lambda peer: signal(barrier, peer))
        for_peers(half, lambda peer: signal(barrier, peer))

    loads = []
    for place, (source, target) in enumerate(
        ((key_ref, key_in), (value_ref, value_in), (query_ref, query_in), (upstream_ref, upstream_in))
    ):
        load = pltpu.make_async_copy(source, target, in_sems.at[place])
        load.start()
        loads.append(load)

    @pl.when(jnp.logical_not(is_first))
    def _():
        pl.semaphore_wait(barrier, members)
        for_peers(0, lambda peer: signal(ready_sem, peer))

    rate = rate_ref[...]
    residue = residue_ref[...]
    spread = (iota((16, LANES), 1) % 16 == iota((16, LANES), 0)).astype(F32)
    own_lane = iota((OWN, LANES), 1) // 16 == iota((OWN, LANES), 0)

    def to_row(params):
        tiled = dot(params, spread, precision=HIGHEST)
        return jnp.sum(jnp.where(own_lane, tiled, 0.0), axis=0, keepdims=True)

    rate_row = to_row(rate)
    gain_row = to_row(residue * jnp.sqrt(rate))

    for load in loads:
        load.wait()
    channels = blocks * OWN
    for first in range(0, channels, LANES):
        cols = pl.ds(first, LANES)
        gated = (key_in[:, cols].astype(F32) * value_in[:, cols].astype(F32)).astype(BF16)
        gate_grad = (upstream_in[:, cols].astype(F32) * query_in[:, cols].astype(F32)).astype(BF16)
        gated = jnp.transpose(gated.astype(F32)).reshape(LANES // OWN, OWN, BLOCK)
        gate_grad = jnp.transpose(gate_grad.astype(F32)).reshape(LANES // OWN, OWN, BLOCK)
        send_a[pl.ds(first // OWN, LANES // OWN)] = jnp.concatenate(
            [gated, gate_grad], axis=1
        ).astype(BF16)

    def push(send, recv, phase, base):
        def one(peer):
            pltpu.make_async_remote_copy(
                src_ref=send.at[peer],
                dst_ref=recv.at[me],
                send_sem=send_sems.at[phase],
                recv_sem=recv_sems.at[phase],
                device_id={"ctx": peer},
                device_id_type=MESH,
            ).start()

        for_peers(base, one)

    def keep(send, recv, phase):
        pltpu.make_async_copy(send.at[me], recv.at[me], recv_sems.at[phase]).start()

    def arrived(recv, phase):
        pltpu.make_async_copy(recv, recv, recv_sems.at[phase]).wait()

    def sent(send, phase):
        rest = send.at[pl.ds(0, blocks - 1)]
        pltpu.make_async_copy(rest, rest, send_sems.at[phase]).wait()

    @pl.when(is_first)
    def _():
        pl.semaphore_wait(barrier, members - 1)

    push(send_a, recv_a, 0, 0)
    keep(send_a, recv_a, 0)

    place_row = iota((BLOCK, LANES), 0).astype(F32)
    place_lane = iota((OWN, LANES), 1).astype(F32)
    ahead = jnp.exp(-rate_row * (float(BLOCK - 1) - place_row))
    behind = jnp.exp(-rate_row * (place_row + 1.0))
    for place, table in enumerate((ahead, behind, gain_row * behind, gain_row * ahead)):
        high, low = split(table)
        tables[2 * place] = high
        tables[2 * place + 1] = low
    taps = jnp.zeros((OWN, LANES), F32)
    for mode in range(16):
        mode_rate = rate[:, mode : mode + 1]
        taps = taps + residue[:, mode : mode + 1] * (
            jnp.sqrt(mode_rate) * jnp.exp(-mode_rate * place_lane)
        )
    causal = iota((BLOCK, BLOCK), 1) >= iota((BLOCK, BLOCK), 0)
    for channel in range(OWN):
        row = jnp.broadcast_to(taps[channel : channel + 1], (BLOCK, LANES))
        row = pltpu.roll(row, 0, 1, stride=1, stride_axis=0)
        high, low = split(jnp.where(causal, row, 0.0))
        toep_hi[channel] = high
        toep_lo[channel] = low

    @pl.when(is_first)
    def _():
        pl.semaphore_wait(ready_sem, members)

        def relay(z):
            signal(relay_sem, (my_y * blocks_z + z) * 2 + my_core)

        @pl.when(my_z == 0)
        def _():
            for z in range(half + half // 2, blocks_z):
                relay(z)

        @pl.when(my_z == half - 1)
        def _():
            for z in range(half, half + half // 2):
                relay(z)

    @pl.when(jnp.logical_not(is_first))
    def _():
        pl.semaphore_wait(relay_sem, 1)

    push(send_a, recv_a, 0, half)

    arrived(recv_a, 0)
    wide[...] = recv_a[...].astype(F32).reshape(blocks * 16, BLOCK)
    for channel in range(OWN):
        rows = pl.ds(channel * blocks, blocks)
        xs[rows, :] = wide[pl.ds(channel, blocks, stride=16), :].astype(BF16)
        gs[rows, :] = wide[pl.ds(OWN + channel, blocks, stride=16), :].astype(BF16)
    x_all = xs[...]
    g_all = gs[...]
    x_ends = own_rows(dot(x_all, tables[0]) + dot(x_all, tables[1]), blocks)
    g_ends = own_rows(dot(g_all, tables[2]) + dot(g_all, tables[3]), blocks)
    x_state = scan_blocks(x_ends, rate_row, True)
    g_state = scan_blocks(g_ends, rate_row, False)
    group = iota((blocks, LANES), 1) // 16

    def carried(state, high, low):
        parts = jnp.concatenate(
            [jnp.where(group == channel, state, 0.0) for channel in range(OWN)], axis=0
        )
        part_hi, part_lo = split(parts)
        over = ((1,), (1,))
        return dot(part_hi, high, over) + dot(part_lo, high, over) + dot(part_hi, low, over)

    x_carried = carried(x_state, tables[4], tables[5])
    g_carried = carried(g_state, tables[6], tables[7])
    for channel in range(OWN):
        rows = slice(channel * blocks, (channel + 1) * blocks)
        x_own = x_all[rows]
        g_own = g_all[rows]
        high = toep_hi[channel]
        low = toep_lo[channel]
        over = ((1,), (1,))
        wide[pl.ds(channel, blocks, stride=16), :] = (
            dot(x_own, high) + dot(x_own, low) + x_carried[rows]
        )
        wide[pl.ds(OWN + channel, blocks, stride=16), :] = (
            dot(g_own, high, over) + dot(g_own, low, over) + g_carried[rows]
        )
    send_b[...] = wide[...].reshape(blocks, 16, BLOCK).astype(BF16)
    push(send_b, recv_b, 1, 0)
    keep(send_b, recv_b, 1)
    push(send_b, recv_b, 1, half)

    high, low = split(ahead * (float(BLOCK - 1) - place_row))
    x_slopes = own_rows(dot(x_all, high) + dot(x_all, low), blocks)
    high, low = split(behind * (place_row + 1.0))
    g_slopes = own_rows(dot(g_all, high) + dot(g_all, low), blocks)
    x_state, x_moment = scan_moments(x_ends, x_slopes, rate_row)
    plain = jnp.sum(g_ends * x_state, axis=0, keepdims=True)
    sloped = jnp.sum(g_ends * x_moment + g_slopes * x_state, axis=0, keepdims=True)
    reverse = (iota((BLOCK, BLOCK), 0) + iota((BLOCK, BLOCK), 1) == BLOCK - 1).astype(BF16)
    x_reversed = dot(x_all, reverse).astype(BF16)
    paired = iota((BLOCK, BLOCK), 0) + iota((BLOCK, BLOCK), 1) >= BLOCK - 1
    lags = []
    for channel in range(OWN):
        rows = slice(channel * blocks, (channel + 1) * blocks)
        pairs = dot(g_all[rows], x_reversed[rows], ((0,), (0,)))
        pairs = jnp.where(paired, pairs, 0.0)
        pairs = pltpu.roll(pairs, 1, 1, stride=1, stride_axis=0)
        lags.append(jnp.sum(pairs, axis=0, keepdims=True))
    lags = jnp.concatenate(lags, axis=0)
    decays = jnp.exp(-rate_row * place_row)

    def own_sum(table):
        full = dot(lags, table, precision=HIGHEST)
        return jnp.sum(jnp.where(own_lane, full, 0.0), axis=0, keepdims=True)

    plain = plain + own_sum(decays)
    sloped = sloped + own_sum(decays * place_row)
    root_row = jnp.sqrt(rate_row) * scale
    residue_row = to_row(residue)
    gather = (iota((LANES, 16), 0) % 16 == iota((LANES, 16), 1)).astype(F32)

    def from_row(row):
        rows = jnp.where(own_lane, jnp.broadcast_to(row, (OWN, LANES)), 0.0)
        return dot(rows, gather, precision=HIGHEST)

    residue_grad_ref[...] = from_row(root_row * plain)
    rate_grad_ref[...] = from_row(root_row * residue_row * (0.5 * plain - rate_row * sloped))

    arrived(recv_b, 1)
    for first in range(0, channels, LANES):
        cols = pl.ds(first, LANES)
        both = recv_b[pl.ds(first // OWN, LANES // OWN)].astype(F32)
        out_ref[:, cols] = jnp.transpose(both[:, :OWN].reshape(LANES, BLOCK)).astype(BF16)
        grad_ref[:, cols] = jnp.transpose(both[:, OWN:].reshape(LANES, BLOCK)).astype(BF16)
    sent(send_a, 0)
    sent(send_b, 1)


def finish(
    upstream_ref,
    value_ref,
    key_ref,
    out_ref,
    grad_ref,
    residue_grad_ref,
    rate_grad_ref,
    query_grad_hbm,
    key_grad_hbm,
    value_grad_hbm,
    residue_grad_hbm,
    rate_grad_hbm,
    query_grad,
    key_grad,
    value_grad,
    out_sems,
):
    stores = [
        pltpu.make_async_copy(source, target, out_sems.at[place])
        for place, (source, target) in enumerate(
            (
                (query_grad, query_grad_hbm),
                (key_grad, key_grad_hbm),
                (value_grad, value_grad_hbm),
                (residue_grad_ref, residue_grad_hbm),
                (rate_grad_ref, rate_grad_hbm),
            )
        )
    ]
    stores[3].start()
    stores[4].start()
    products = (
        (upstream_ref, out_ref, query_grad),
        (value_ref, grad_ref, key_grad),
        (key_ref, grad_ref, value_grad),
    )
    for store, (gate, result, target) in zip(stores, products):
        target[...] = (gate[...].astype(F32) * result[...].astype(F32)).astype(BF16)
        store.start()
    for store in stores:
        store.wait()


def local(sizes, query_proj, key_proj, value_proj, output_grad, residue, decay_rate):
    tok_dev, channels = query_proj.shape
    blocks = sizes[0] * sizes[1] * 2
    scale = float(tok_dev * blocks) ** (-0.5)
    anywhere = pl.BlockSpec(memory_space=pl.ANY)
    vmem = pl.BlockSpec(memory_space=pltpu.VMEM)
    tokens = jax.ShapeDtypeStruct((tok_dev, channels), BF16)
    params = jax.ShapeDtypeStruct(residue.shape, F32)
    message = pltpu.VMEM((blocks, 16, BLOCK), BF16)
    tokens_vmem = pltpu.VMEM(tokens.shape, BF16)
    params_vmem = pltpu.VMEM(params.shape, F32)
    conv_out, conv_grad, residue_grad, rate_grad = pl.pallas_call(
        functools.partial(kernel, sizes, scale),
        out_shape=(tokens_vmem, tokens_vmem, params_vmem, params_vmem),
        in_specs=[anywhere] * 4 + [vmem] * 2,
        out_specs=[vmem] * 4,
        scratch_shapes=[pltpu.VMEM((tok_dev, channels), BF16)] * 4
        + [message] * 4
        + [
            pltpu.VMEM((blocks * 16, BLOCK), F32),
            pltpu.VMEM((blocks * OWN, BLOCK), BF16),
            pltpu.VMEM((blocks * OWN, BLOCK), BF16),
            pltpu.VMEM((OWN, BLOCK, BLOCK), BF16),
            pltpu.VMEM((OWN, BLOCK, BLOCK), BF16),
            pltpu.VMEM((8, BLOCK, LANES), BF16),
            pltpu.SemaphoreType.DMA((4,)),
            pltpu.SemaphoreType.DMA((2,)),
            pltpu.SemaphoreType.DMA((2,)),
            pltpu.SemaphoreType.REGULAR,
            pltpu.SemaphoreType.REGULAR,
        ],
        compiler_params=pltpu.CompilerParams(collective_id=0, has_side_effects=True, vmem_limit_bytes=60 * 1024 * 1024),
    )(query_proj, key_proj, value_proj, output_grad, residue, decay_rate)
    return pl.pallas_call(
        finish,
        out_shape=(tokens,) * 3 + (params,) * 2,
        in_specs=[vmem] * 7,
        out_specs=[anywhere] * 5,
        scratch_shapes=[pltpu.VMEM((tok_dev, channels), BF16)] * 3
        + [pltpu.SemaphoreType.DMA((5,))],
        compiler_params=pltpu.CompilerParams(vmem_limit_bytes=8 << 20),
    )(output_grad, value_proj, key_proj, conv_out, conv_grad, residue_grad, rate_grad)


def solution(mesh):
    ranks = mesh.shape["ctx"]
    along_z = min(8, ranks // 2)
    sizes = (ranks // (2 * along_z), along_z)
    tokens = P("ctx", "ch")
    params = P(("ch", "ctx"), None)
    return jax.shard_map(
        functools.partial(local, sizes),
        mesh=mesh,
        in_specs=(tokens,) * 4 + (params,) * 2,
        out_specs=(tokens,) * 3 + (params,) * 2,
        check_vma=False,
    )
```

```python
import functools
import math

import jax
import jax.numpy as jnp
from jax import lax
from jax.experimental import pallas as pl
from jax.experimental.pallas import tpu as pltpu
from jax.sharding import PartitionSpec as P

MESH = pl.DeviceIdType.MESH
F32 = jnp.float32
BF16 = jnp.bfloat16
HIGHEST = lax.Precision.HIGHEST
BLOCK = 128
OWN = 8
LANES = 128


def dot(left, right, dims=((1,), (0,)), precision=None):
    return lax.dot_general(
        left, right, (dims, ((), ())), precision=precision, preferred_element_type=F32
    )


def split(value):
    high = value.astype(BF16)
    return high, (value - high.astype(F32)).astype(BF16)


def iota(shape, axis):
    return lax.broadcasted_iota(jnp.int32, shape, axis)


def shift_rows(value, step, down):
    rows = value.shape[0]
    index = iota(value.shape, 0)
    if down:
        return jnp.where(index >= step, pltpu.roll(value, step, 0), 0.0)
    return jnp.where(index < rows - step, pltpu.roll(value, rows - step, 0), 0.0)


def scan_blocks(state, rate_row, down):
    step = 1
    while step < state.shape[0]:
        decay = jnp.exp(rate_row * (-float(BLOCK * step)))
        state = state + decay * shift_rows(state, step, down)
        step *= 2
    return shift_rows(state, 1, down)


def scan_moments(state, moment, rate_row):
    step = 1
    while step < state.shape[0]:
        decay = jnp.exp(rate_row * (-float(BLOCK * step)))
        below = shift_rows(state, step, True)
        moment = moment + decay * (
            shift_rows(moment, step, True) + float(BLOCK * step) * below
        )
        state = state + decay * below
        step *= 2
    return shift_rows(state, 1, True), shift_rows(moment, 1, True)


def own_rows(stacked, blocks):
    group = iota((blocks, LANES), 1) // 16
    total = jnp.zeros((blocks, LANES), F32)
    for channel in range(OWN):
        part = stacked[channel * blocks : (channel + 1) * blocks]
        total = jnp.where(group == channel, part, total)
    return total


def kernel(
    sizes,
    scale,
    query_ref,
    key_ref,
    value_ref,
    upstream_ref,
    residue_ref,
    rate_ref,
    out_ref,
    grad_ref,
    residue_grad_ref,
    rate_grad_ref,
    query_in,
    key_in,
    value_in,
    upstream_in,
    send_a,
    recv_a,
    send_b,
    recv_b,
    wide,
    xs,
    gs,
    toep_hi,
    toep_lo,
    tables,
    in_sems,
    send_sems,
    recv_sems,
):
    blocks_y, blocks_z = sizes
    blocks = blocks_y * blocks_z * 2
    me = lax.axis_index("ctx")
    my_core = lax.rem(me, 2)
    my_z = lax.rem(me // 2, blocks_z)
    my_y = me // (2 * blocks_z)

    half = blocks_z // 2

    def for_plane(plane, action):
        for step in range(2 * blocks_y):
            y = lax.rem(my_y + step // 2, blocks_y)
            core = lax.rem(my_core + step, 2)
            peer = (y * blocks_z + plane) * 2 + core
            if step == 0:
                pl.when(plane != my_z)(functools.partial(action, peer))
            else:
                action(peer)

    def for_far_first(action):
        def one(step, carry):
            delta = (1 - 2 * lax.rem(step, 2)) * ((step + 1) // 2)
            for_plane(lax.rem(my_z + half + delta + blocks_z, blocks_z), action)
            return carry

        lax.fori_loop(0, blocks_z, one, 0)

    def for_planes(first, last, action):
        def one(plane, carry):
            for_plane(plane, action)
            return carry

        lax.fori_loop(first, last, one, 0)

    barrier = pltpu.get_barrier_semaphore()

    def greet(peer):
        pl.semaphore_signal(barrier, inc=1, device_id={"ctx": peer}, device_id_type=MESH)

    for_far_first(greet)

    loads = []
    for place, (source, target) in enumerate(
        ((key_ref, key_in), (value_ref, value_in), (query_ref, query_in), (upstream_ref, upstream_in))
    ):
        load = pltpu.make_async_copy(source, target, in_sems.at[place])
        load.start()
        loads.append(load)

    rate = rate_ref[...]
    residue = residue_ref[...]
    spread = (iota((16, LANES), 1) % 16 == iota((16, LANES), 0)).astype(F32)
    own_lane = iota((OWN, LANES), 1) // 16 == iota((OWN, LANES), 0)

    def to_row(params):
        tiled = dot(params, spread, precision=HIGHEST)
        return jnp.sum(jnp.where(own_lane, tiled, 0.0), axis=0, keepdims=True)

    rate_row = to_row(rate)
    gain_row = to_row(residue * jnp.sqrt(rate))

    channels = blocks * OWN
    for array, (left, right) in enumerate(((key_in, value_in), (upstream_in, query_in))):
        loads[2 * array].wait()
        loads[2 * array + 1].wait()
        for first in range(0, channels, LANES):
            cols = pl.ds(first, LANES)
            product = (left[:, cols].astype(F32) * right[:, cols].astype(F32)).astype(BF16)
            send_a[array, pl.ds(first // OWN, LANES // OWN)] = (
                jnp.transpose(product.astype(F32)).reshape(LANES // OWN, OWN, BLOCK).astype(BF16)
            )

    pl.semaphore_wait(barrier, blocks - 1)

    def pusher(send, recv, phase, array):
        def push(peer):
            pltpu.make_async_remote_copy(
                src_ref=send.at[array, peer],
                dst_ref=recv.at[array, me],
                send_sem=send_sems.at[phase, array],
                recv_sem=recv_sems.at[phase, array],
                device_id={"ctx": peer},
                device_id_type=MESH,
            ).start()

        return push

    def keep(send, recv, phase, array):
        pltpu.make_async_copy(
            send.at[array, me], recv.at[array, me], recv_sems.at[phase, array]
        ).start()

    def arrived(recv, phase, array):
        pltpu.make_async_copy(recv.at[array], recv.at[array], recv_sems.at[phase, array]).wait()

    def sent(send, phase, array):
        rest = send.at[array, pl.ds(0, blocks - 1)]
        pltpu.make_async_copy(rest, rest, send_sems.at[phase, array]).wait()

    for array in range(2):
        for_far_first(pusher(send_a, recv_a, 0, array))
        keep(send_a, recv_a, 0, array)

    place_row = iota((BLOCK, LANES), 0).astype(F32)
    place_lane = iota((OWN, LANES), 1).astype(F32)
    ahead = jnp.exp(-rate_row * (float(BLOCK - 1) - place_row))
    behind = jnp.exp(-rate_row * (place_row + 1.0))
    for place, table in enumerate((ahead, behind, gain_row * behind, gain_row * ahead)):
        high, low = split(table)
        tables[2 * place] = high
        tables[2 * place + 1] = low
    taps = jnp.zeros((OWN, LANES), F32)
    for mode in range(16):
        mode_rate = rate[:, mode : mode + 1]
        taps = taps + residue[:, mode : mode + 1] * (
            jnp.sqrt(mode_rate) * jnp.exp(-mode_rate * place_lane)
        )
    causal = iota((BLOCK, BLOCK), 1) >= iota((BLOCK, BLOCK), 0)
    for channel in range(OWN):
        row = jnp.broadcast_to(taps[channel : channel + 1], (BLOCK, LANES))
        row = pltpu.roll(row, 0, 1, stride=1, stride_axis=0)
        high, low = split(jnp.where(causal, row, 0.0))
        toep_hi[channel] = high
        toep_lo[channel] = low

    group = iota((blocks, LANES), 1) // 16

    def own_signals(array, target):
        arrived(recv_a, 0, array)
        wide[...] = recv_a[array].astype(F32).reshape(blocks * OWN, BLOCK)
        for channel in range(OWN):
            target[pl.ds(channel * blocks, blocks), :] = wide[
                pl.ds(channel, blocks, stride=OWN), :
            ].astype(BF16)
        return target[...]

    def respond(array, signals, state, table, over):
        high, low = tables[table], tables[table + 1]
        parts = jnp.concatenate(
            [jnp.where(group == channel, state, 0.0) for channel in range(OWN)], axis=0
        )
        part_hi, part_lo = split(parts)
        lanes = ((1,), (1,))
        carried = dot(part_hi, high, lanes) + dot(part_lo, high, lanes) + dot(part_hi, low, lanes)
        for channel in range(OWN):
            rows = slice(channel * blocks, (channel + 1) * blocks)
            wide[pl.ds(channel, blocks, stride=OWN), :] = (
                dot(signals[rows], toep_hi[channel], over)
                + dot(signals[rows], toep_lo[channel], over)
                + carried[rows]
            )
        send_b[array] = wide[...].reshape(blocks, OWN, BLOCK).astype(BF16)

    x_all = own_signals(0, xs)
    x_ends = own_rows(dot(x_all, tables[0]) + dot(x_all, tables[1]), blocks)
    x_state = scan_blocks(x_ends, rate_row, True)
    respond(0, x_all, x_state, 4, ((1,), (0,)))
    for_far_first(pusher(send_b, recv_b, 1, 0))
    keep(send_b, recv_b, 1, 0)

    g_all = own_signals(1, gs)
    g_ends = own_rows(dot(g_all, tables[2]) + dot(g_all, tables[3]), blocks)
    g_state = scan_blocks(g_ends, rate_row, False)
    respond(1, g_all, g_state, 6, ((1,), (1,)))
    for_far_first(pusher(send_b, recv_b, 1, 1))
    keep(send_b, recv_b, 1, 1)

    high, low = split(ahead * (float(BLOCK - 1) - place_row))
    x_slopes = own_rows(dot(x_all, high) + dot(x_all, low), blocks)
    high, low = split(behind * (place_row + 1.0))
    g_slopes = own_rows(dot(g_all, high) + dot(g_all, low), blocks)
    x_state, x_moment = scan_moments(x_ends, x_slopes, rate_row)
    plain = jnp.sum(g_ends * x_state, axis=0, keepdims=True)
    sloped = jnp.sum(g_ends * x_moment + g_slopes * x_state, axis=0, keepdims=True)
    reverse = (iota((BLOCK, BLOCK), 0) + iota((BLOCK, BLOCK), 1) == BLOCK - 1).astype(BF16)
    x_reversed = dot(x_all, reverse).astype(BF16)
    paired = iota((BLOCK, BLOCK), 0) + iota((BLOCK, BLOCK), 1) >= BLOCK - 1
    lags = []
    for channel in range(OWN):
        rows = slice(channel * blocks, (channel + 1) * blocks)
        pairs = dot(g_all[rows], x_reversed[rows], ((0,), (0,)))
        pairs = jnp.where(paired, pairs, 0.0)
        pairs = pltpu.roll(pairs, 1, 1, stride=1, stride_axis=0)
        lags.append(jnp.sum(pairs, axis=0, keepdims=True))
    lags = jnp.concatenate(lags, axis=0)
    decays = jnp.exp(-rate_row * place_row)

    def own_sum(table):
        full = dot(lags, table, precision=HIGHEST)
        return jnp.sum(jnp.where(own_lane, full, 0.0), axis=0, keepdims=True)

    plain = plain + own_sum(decays)
    sloped = sloped + own_sum(decays * place_row)
    root_row = jnp.sqrt(rate_row) * scale
    residue_row = to_row(residue)
    gather = (iota((LANES, 16), 0) % 16 == iota((LANES, 16), 1)).astype(F32)

    def from_row(row):
        rows = jnp.where(own_lane, jnp.broadcast_to(row, (OWN, LANES)), 0.0)
        return dot(rows, gather, precision=HIGHEST)

    residue_grad_ref[...] = from_row(root_row * plain)
    rate_grad_ref[...] = from_row(root_row * residue_row * (0.5 * plain - rate_row * sloped))

    for array, target in enumerate((out_ref, grad_ref)):
        arrived(recv_b, 1, array)
        for first in range(0, channels, LANES):
            part = recv_b[array, pl.ds(first // OWN, LANES // OWN)].astype(F32)
            target[:, pl.ds(first, LANES)] = jnp.transpose(part.reshape(LANES, BLOCK)).astype(BF16)
    for array in range(2):
        sent(send_a, 0, array)
        sent(send_b, 1, array)


def finish(
    upstream_ref,
    value_ref,
    key_ref,
    out_ref,
    grad_ref,
    residue_grad_ref,
    rate_grad_ref,
    query_grad_hbm,
    key_grad_hbm,
    value_grad_hbm,
    residue_grad_hbm,
    rate_grad_hbm,
    query_grad,
    key_grad,
    value_grad,
    out_sems,
):
    stores = [
        pltpu.make_async_copy(source, target, out_sems.at[place])
        for place, (source, target) in enumerate(
            (
                (query_grad, query_grad_hbm),
                (key_grad, key_grad_hbm),
                (value_grad, value_grad_hbm),
                (residue_grad_ref, residue_grad_hbm),
                (rate_grad_ref, rate_grad_hbm),
            )
        )
    ]
    stores[3].start()
    stores[4].start()
    products = (
        (upstream_ref, out_ref, query_grad),
        (value_ref, grad_ref, key_grad),
        (key_ref, grad_ref, value_grad),
    )
    for store, (gate, result, target) in zip(stores, products):
        target[...] = (gate[...].astype(F32) * result[...].astype(F32)).astype(BF16)
        store.start()
    for store in stores:
        store.wait()


def local(sizes, query_proj, key_proj, value_proj, output_grad, residue, decay_rate):
    tok_dev, channels = query_proj.shape
    blocks = sizes[0] * sizes[1] * 2
    scale = float(tok_dev * blocks) ** (-0.5)
    anywhere = pl.BlockSpec(memory_space=pl.ANY)
    vmem = pl.BlockSpec(memory_space=pltpu.VMEM)
    tokens = jax.ShapeDtypeStruct((tok_dev, channels), BF16)
    params = jax.ShapeDtypeStruct(residue.shape, F32)
    message = pltpu.VMEM((2, blocks, OWN, BLOCK), BF16)
    tokens_vmem = pltpu.VMEM(tokens.shape, BF16)
    params_vmem = pltpu.VMEM(params.shape, F32)
    conv_out, conv_grad, residue_grad, rate_grad = pl.pallas_call(
        functools.partial(kernel, sizes, scale),
        out_shape=(tokens_vmem, tokens_vmem, params_vmem, params_vmem),
        in_specs=[anywhere] * 4 + [vmem] * 2,
        out_specs=[vmem] * 4,
        scratch_shapes=[pltpu.VMEM((tok_dev, channels), BF16)] * 4
        + [message] * 4
        + [
            pltpu.VMEM((blocks * OWN, BLOCK), F32),
            pltpu.VMEM((blocks * OWN, BLOCK), BF16),
            pltpu.VMEM((blocks * OWN, BLOCK), BF16),
            pltpu.VMEM((OWN, BLOCK, BLOCK), BF16),
            pltpu.VMEM((OWN, BLOCK, BLOCK), BF16),
            pltpu.VMEM((8, BLOCK, LANES), BF16),
            pltpu.SemaphoreType.DMA((4,)),
            pltpu.SemaphoreType.DMA((2, 2)),
            pltpu.SemaphoreType.DMA((2, 2)),
        ],
        compiler_params=pltpu.CompilerParams(collective_id=0, has_side_effects=True, vmem_limit_bytes=60 * 1024 * 1024),
    )(query_proj, key_proj, value_proj, output_grad, residue, decay_rate)
    return pl.pallas_call(
        finish,
        out_shape=(tokens,) * 3 + (params,) * 2,
        in_specs=[vmem] * 7,
        out_specs=[anywhere] * 5,
        scratch_shapes=[pltpu.VMEM((tok_dev, channels), BF16)] * 3
        + [pltpu.SemaphoreType.DMA((5,))],
        compiler_params=pltpu.CompilerParams(vmem_limit_bytes=8 << 20),
    )(output_grad, value_proj, key_proj, conv_out, conv_grad, residue_grad, rate_grad)


def solution(mesh):
    ranks = mesh.shape["ctx"]
    along_z = min(8, ranks // 2)
    sizes = (ranks // (2 * along_z), along_z)
    tokens = P("ctx", "ch")
    params = P(("ch", "ctx"), None)
    return jax.shard_map(
        functools.partial(local, sizes),
        mesh=mesh,
        in_specs=(tokens,) * 4 + (params,) * 2,
        out_specs=(tokens,) * 3 + (params,) * 2,
        check_vma=False,
    )
```

```python
import functools
import math

import jax
import jax.numpy as jnp
from jax import lax
from jax.experimental import pallas as pl
from jax.experimental.pallas import tpu as pltpu
from jax.sharding import PartitionSpec as P

MESH = pl.DeviceIdType.MESH
F32 = jnp.float32
BF16 = jnp.bfloat16
HIGHEST = lax.Precision.HIGHEST
BLOCK = 128
OWN = 8
LANES = 128


def dot(left, right, dims=((1,), (0,)), precision=None):
    return lax.dot_general(
        left, right, (dims, ((), ())), precision=precision, preferred_element_type=F32
    )


def split(value):
    high = value.astype(BF16)
    return high, (value - high.astype(F32)).astype(BF16)


def iota(shape, axis):
    return lax.broadcasted_iota(jnp.int32, shape, axis)


def shift_rows(value, step, down):
    rows = value.shape[0]
    index = iota(value.shape, 0)
    if down:
        return jnp.where(index >= step, pltpu.roll(value, step, 0), 0.0)
    return jnp.where(index < rows - step, pltpu.roll(value, rows - step, 0), 0.0)


def scan_blocks(state, rate_row, down):
    step = 1
    while step < state.shape[0]:
        decay = jnp.exp(rate_row * (-float(BLOCK * step)))
        state = state + decay * shift_rows(state, step, down)
        step *= 2
    return shift_rows(state, 1, down)


def scan_moments(state, moment, rate_row):
    step = 1
    while step < state.shape[0]:
        decay = jnp.exp(rate_row * (-float(BLOCK * step)))
        below = shift_rows(state, step, True)
        moment = moment + decay * (
            shift_rows(moment, step, True) + float(BLOCK * step) * below
        )
        state = state + decay * below
        step *= 2
    return shift_rows(state, 1, True), shift_rows(moment, 1, True)


def own_rows(stacked, blocks):
    group = iota((blocks, LANES), 1) // 16
    total = jnp.zeros((blocks, LANES), F32)
    for channel in range(OWN):
        part = stacked[channel * blocks : (channel + 1) * blocks]
        total = jnp.where(group == channel, part, total)
    return total


def kernel(
    sizes,
    scale,
    query_ref,
    key_ref,
    value_ref,
    upstream_ref,
    residue_ref,
    rate_ref,
    query_grad_ref,
    key_grad_ref,
    value_grad_ref,
    residue_grad_ref,
    rate_grad_ref,
    query_in,
    key_in,
    value_in,
    upstream_in,
    residue_in,
    rate_in,
    send_a,
    recv_a,
    send_b,
    recv_b,
    wide,
    xs,
    gs,
    toep_hi,
    toep_lo,
    tables,
    in_sems,
    send_sems,
    recv_sems,
):
    blocks_y, blocks_z = sizes
    blocks = blocks_y * blocks_z * 2
    me = lax.axis_index("ctx")
    my_core = lax.rem(me, 2)
    my_z = lax.rem(me // 2, blocks_z)
    my_y = me // (2 * blocks_z)

    half = blocks_z // 2

    def for_plane(plane, action):
        for step in range(2 * blocks_y):
            y = lax.rem(my_y + step // 2, blocks_y)
            core = lax.rem(my_core + step, 2)
            peer = (y * blocks_z + plane) * 2 + core
            if step == 0:
                pl.when(plane != my_z)(functools.partial(action, peer))
            else:
                action(peer)

    def for_far_first(action):
        def one(step, carry):
            delta = (1 - 2 * lax.rem(step, 2)) * ((step + 1) // 2)
            for_plane(lax.rem(my_z + half + delta + blocks_z, blocks_z), action)
            return carry

        lax.fori_loop(0, blocks_z, one, 0)

    def for_planes(first, last, action):
        def one(plane, carry):
            for_plane(plane, action)
            return carry

        lax.fori_loop(first, last, one, 0)

    barrier = pltpu.get_barrier_semaphore()

    def greet(peer):
        pl.semaphore_signal(barrier, inc=1, device_id={"ctx": peer}, device_id_type=MESH)

    for_far_first(greet)

    loads = []
    for place, (source, target) in enumerate(
        (
            (key_ref, key_in),
            (value_ref, value_in),
            (query_ref, query_in),
            (upstream_ref, upstream_in),
            (residue_ref, residue_in),
            (rate_ref, rate_in),
        )
    ):
        load = pltpu.make_async_copy(source, target, in_sems.at[place])
        load.start()
        loads.append(load)

    loads[4].wait()
    loads[5].wait()
    rate = rate_in[...]
    residue = residue_in[...]
    spread = (iota((16, LANES), 1) % 16 == iota((16, LANES), 0)).astype(F32)
    own_lane = iota((OWN, LANES), 1) // 16 == iota((OWN, LANES), 0)

    def to_row(params):
        tiled = dot(params, spread, precision=HIGHEST)
        return jnp.sum(jnp.where(own_lane, tiled, 0.0), axis=0, keepdims=True)

    rate_row = to_row(rate)
    gain_row = to_row(residue * jnp.sqrt(rate))

    channels = blocks * OWN
    for array, (left, right) in enumerate(((key_in, value_in), (upstream_in, query_in))):
        loads[2 * array].wait()
        loads[2 * array + 1].wait()
        for first in range(0, channels, LANES):
            cols = pl.ds(first, LANES)
            product = (left[:, cols].astype(F32) * right[:, cols].astype(F32)).astype(BF16)
            send_a[array, pl.ds(first // OWN, LANES // OWN)] = (
                jnp.transpose(product.astype(F32)).reshape(LANES // OWN, OWN, BLOCK).astype(BF16)
            )

    pl.semaphore_wait(barrier, blocks - 1)

    def pusher(send, recv, phase, array):
        def push(peer):
            pltpu.make_async_remote_copy(
                src_ref=send.at[array, peer],
                dst_ref=recv.at[array, me],
                send_sem=send_sems.at[phase, array],
                recv_sem=recv_sems.at[phase, array],
                device_id={"ctx": peer},
                device_id_type=MESH,
            ).start()

        return push

    def keep(send, recv, phase, array):
        pltpu.make_async_copy(
            send.at[array, me], recv.at[array, me], recv_sems.at[phase, array]
        ).start()

    def arrived(recv, phase, array):
        pltpu.make_async_copy(recv.at[array], recv.at[array], recv_sems.at[phase, array]).wait()

    def sent(send, phase, array):
        rest = send.at[array, pl.ds(0, blocks - 1)]
        pltpu.make_async_copy(rest, rest, send_sems.at[phase, array]).wait()

    for array in range(2):
        for_far_first(pusher(send_a, recv_a, 0, array))
        keep(send_a, recv_a, 0, array)

    place_row = iota((BLOCK, LANES), 0).astype(F32)
    place_lane = iota((OWN, LANES), 1).astype(F32)
    ahead = jnp.exp(-rate_row * (float(BLOCK - 1) - place_row))
    behind = jnp.exp(-rate_row * (place_row + 1.0))
    for place, table in enumerate((ahead, behind, gain_row * behind, gain_row * ahead)):
        high, low = split(table)
        tables[2 * place] = high
        tables[2 * place + 1] = low
    taps = jnp.zeros((OWN, LANES), F32)
    for mode in range(16):
        mode_rate = rate[:, mode : mode + 1]
        taps = taps + residue[:, mode : mode + 1] * (
            jnp.sqrt(mode_rate) * jnp.exp(-mode_rate * place_lane)
        )
    causal = iota((BLOCK, BLOCK), 1) >= iota((BLOCK, BLOCK), 0)
    for channel in range(OWN):
        row = jnp.broadcast_to(taps[channel : channel + 1], (BLOCK, LANES))
        row = pltpu.roll(row, 0, 1, stride=1, stride_axis=0)
        high, low = split(jnp.where(causal, row, 0.0))
        toep_hi[channel] = high
        toep_lo[channel] = low

    group = iota((blocks, LANES), 1) // 16

    def own_signals(array, target):
        arrived(recv_a, 0, array)
        wide[...] = recv_a[array].astype(F32).reshape(blocks * OWN, BLOCK)
        for channel in range(OWN):
            target[pl.ds(channel * blocks, blocks), :] = wide[
                pl.ds(channel, blocks, stride=OWN), :
            ].astype(BF16)
        return target[...]

    def respond(array, signals, state, table, over):
        high, low = tables[table], tables[table + 1]
        parts = jnp.concatenate(
            [jnp.where(group == channel, state, 0.0) for channel in range(OWN)], axis=0
        )
        part_hi, part_lo = split(parts)
        lanes = ((1,), (1,))
        carried = dot(part_hi, high, lanes) + dot(part_lo, high, lanes) + dot(part_hi, low, lanes)
        for channel in range(OWN):
            rows = slice(channel * blocks, (channel + 1) * blocks)
            wide[pl.ds(channel, blocks, stride=OWN), :] = (
                dot(signals[rows], toep_hi[channel], over)
                + dot(signals[rows], toep_lo[channel], over)
                + carried[rows]
            )
        send_b[array] = wide[...].reshape(blocks, OWN, BLOCK).astype(BF16)

    x_all = own_signals(0, xs)
    x_ends = own_rows(dot(x_all, tables[0]) + dot(x_all, tables[1]), blocks)
    x_state = scan_blocks(x_ends, rate_row, True)
    respond(0, x_all, x_state, 4, ((1,), (0,)))
    for_far_first(pusher(send_b, recv_b, 1, 0))
    keep(send_b, recv_b, 1, 0)

    g_all = own_signals(1, gs)
    g_ends = own_rows(dot(g_all, tables[2]) + dot(g_all, tables[3]), blocks)
    g_state = scan_blocks(g_ends, rate_row, False)
    respond(1, g_all, g_state, 6, ((1,), (1,)))
    for_far_first(pusher(send_b, recv_b, 1, 1))
    keep(send_b, recv_b, 1, 1)

    high, low = split(ahead * (float(BLOCK - 1) - place_row))
    x_slopes = own_rows(dot(x_all, high) + dot(x_all, low), blocks)
    high, low = split(behind * (place_row + 1.0))
    g_slopes = own_rows(dot(g_all, high) + dot(g_all, low), blocks)
    x_state, x_moment = scan_moments(x_ends, x_slopes, rate_row)
    plain = jnp.sum(g_ends * x_state, axis=0, keepdims=True)
    sloped = jnp.sum(g_ends * x_moment + g_slopes * x_state, axis=0, keepdims=True)
    reverse = (iota((BLOCK, BLOCK), 0) + iota((BLOCK, BLOCK), 1) == BLOCK - 1).astype(BF16)
    x_reversed = dot(x_all, reverse).astype(BF16)
    paired = iota((BLOCK, BLOCK), 0) + iota((BLOCK, BLOCK), 1) >= BLOCK - 1
    lags = []
    for channel in range(OWN):
        rows = slice(channel * blocks, (channel + 1) * blocks)
        pairs = dot(g_all[rows], x_reversed[rows], ((0,), (0,)))
        pairs = jnp.where(paired, pairs, 0.0)
        pairs = pltpu.roll(pairs, 1, 1, stride=1, stride_axis=0)
        lags.append(jnp.sum(pairs, axis=0, keepdims=True))
    lags = jnp.concatenate(lags, axis=0)
    decays = jnp.exp(-rate_row * place_row)

    def own_sum(table):
        full = dot(lags, table, precision=HIGHEST)
        return jnp.sum(jnp.where(own_lane, full, 0.0), axis=0, keepdims=True)

    plain = plain + own_sum(decays)
    sloped = sloped + own_sum(decays * place_row)
    root_row = jnp.sqrt(rate_row) * scale
    residue_row = to_row(residue)
    gather = (iota((LANES, 16), 0) % 16 == iota((LANES, 16), 1)).astype(F32)

    def from_row(row):
        rows = jnp.where(own_lane, jnp.broadcast_to(row, (OWN, LANES)), 0.0)
        return dot(rows, gather, precision=HIGHEST)

    residue_grad_ref[...] = from_row(root_row * plain)
    rate_grad_ref[...] = from_row(root_row * residue_row * (0.5 * plain - rate_row * sloped))

    products = (
        ((upstream_in, query_grad_ref),),
        ((value_in, key_grad_ref), (key_in, value_grad_ref)),
    )
    for array in range(2):
        arrived(recv_b, 1, array)
        for first in range(0, channels, LANES):
            cols = pl.ds(first, LANES)
            part = recv_b[array, pl.ds(first // OWN, LANES // OWN)].astype(F32)
            part = jnp.transpose(part.reshape(LANES, BLOCK))
            for gate, target in products[array]:
                target[:, cols] = (gate[:, cols].astype(F32) * part).astype(BF16)
    for array in range(2):
        sent(send_a, 0, array)
        sent(send_b, 1, array)


def finish(*refs):
    count = len(refs) // 2
    sources, targets, sems = refs[:count], refs[count:-1], refs[-1]
    stores = [
        pltpu.make_async_copy(source, target, sems.at[place])
        for place, (source, target) in enumerate(zip(sources, targets))
    ]
    for store in stores:
        store.start()
    for store in stores:
        store.wait()


def local(sizes, query_proj, key_proj, value_proj, output_grad, residue, decay_rate):
    tok_dev, channels = query_proj.shape
    blocks = sizes[0] * sizes[1] * 2
    scale = float(tok_dev * blocks) ** (-0.5)
    anywhere = pl.BlockSpec(memory_space=pl.ANY)
    vmem = pl.BlockSpec(memory_space=pltpu.VMEM)
    tokens = jax.ShapeDtypeStruct((tok_dev, channels), BF16)
    params = jax.ShapeDtypeStruct(residue.shape, F32)
    message = pltpu.VMEM((2, blocks, OWN, BLOCK), BF16)
    tokens_vmem = pltpu.VMEM(tokens.shape, BF16)
    params_vmem = pltpu.VMEM(params.shape, F32)
    results = pl.pallas_call(
        functools.partial(kernel, sizes, scale),
        out_shape=(tokens_vmem,) * 3 + (params_vmem,) * 2,
        in_specs=[anywhere] * 6,
        out_specs=[vmem] * 5,
        scratch_shapes=[pltpu.VMEM((tok_dev, channels), BF16)] * 4
        + [params_vmem] * 2
        + [message] * 4
        + [
            pltpu.VMEM((blocks * OWN, BLOCK), F32),
            pltpu.VMEM((blocks * OWN, BLOCK), BF16),
            pltpu.VMEM((blocks * OWN, BLOCK), BF16),
            pltpu.VMEM((OWN, BLOCK, BLOCK), BF16),
            pltpu.VMEM((OWN, BLOCK, BLOCK), BF16),
            pltpu.VMEM((8, BLOCK, LANES), BF16),
            pltpu.SemaphoreType.DMA((6,)),
            pltpu.SemaphoreType.DMA((2, 2)),
            pltpu.SemaphoreType.DMA((2, 2)),
        ],
        compiler_params=pltpu.CompilerParams(collective_id=0, has_side_effects=True, vmem_limit_bytes=60 * 1024 * 1024),
    )(query_proj, key_proj, value_proj, output_grad, residue, decay_rate)
    return pl.pallas_call(
        finish,
        out_shape=(tokens,) * 3 + (params,) * 2,
        in_specs=[vmem] * 5,
        out_specs=[anywhere] * 5,
        scratch_shapes=[pltpu.SemaphoreType.DMA((5,))],
        compiler_params=pltpu.CompilerParams(vmem_limit_bytes=8 << 20),
    )(*results)


def solution(mesh):
    ranks = mesh.shape["ctx"]
    along_z = min(8, ranks // 2)
    sizes = (ranks // (2 * along_z), along_z)
    tokens = P("ctx", "ch")
    params = P(("ch", "ctx"), None)
    return jax.shard_map(
        functools.partial(local, sizes),
        mesh=mesh,
        in_specs=(tokens,) * 4 + (params,) * 2,
        out_specs=(tokens,) * 3 + (params,) * 2,
        check_vma=False,
    )
```

```python
import functools
import math

import jax
import jax.numpy as jnp
from jax import lax
from jax.experimental import pallas as pl
from jax.experimental.pallas import tpu as pltpu
from jax.sharding import PartitionSpec as P

MESH = pl.DeviceIdType.MESH
F32 = jnp.float32
BF16 = jnp.bfloat16
HIGHEST = lax.Precision.HIGHEST
BLOCK = 128
OWN = 8
LANES = 128


def dot(left, right, dims=((1,), (0,)), precision=None):
    return lax.dot_general(
        left, right, (dims, ((), ())), precision=precision, preferred_element_type=F32
    )


def split(value):
    high = value.astype(BF16)
    return high, (value - high.astype(F32)).astype(BF16)


def iota(shape, axis):
    return lax.broadcasted_iota(jnp.int32, shape, axis)


def shift_rows(value, step, down):
    rows = value.shape[0]
    index = iota(value.shape, 0)
    if down:
        return jnp.where(index >= step, pltpu.roll(value, step, 0), 0.0)
    return jnp.where(index < rows - step, pltpu.roll(value, rows - step, 0), 0.0)


def scan_blocks(state, rate_row, down):
    step = 1
    while step < state.shape[0]:
        decay = jnp.exp(rate_row * (-float(BLOCK * step)))
        state = state + decay * shift_rows(state, step, down)
        step *= 2
    return shift_rows(state, 1, down)


def scan_moments(state, moment, rate_row):
    step = 1
    while step < state.shape[0]:
        decay = jnp.exp(rate_row * (-float(BLOCK * step)))
        below = shift_rows(state, step, True)
        moment = moment + decay * (
            shift_rows(moment, step, True) + float(BLOCK * step) * below
        )
        state = state + decay * below
        step *= 2
    return shift_rows(state, 1, True), shift_rows(moment, 1, True)


def own_rows(stacked, blocks):
    group = iota((blocks, LANES), 1) // 16
    total = jnp.zeros((blocks, LANES), F32)
    for channel in range(OWN):
        part = stacked[channel * blocks : (channel + 1) * blocks]
        total = jnp.where(group == channel, part, total)
    return total


def kernel(
    sizes,
    scale,
    query_ref,
    key_ref,
    value_ref,
    upstream_ref,
    residue_ref,
    rate_ref,
    query_grad_ref,
    key_grad_ref,
    value_grad_ref,
    residue_grad_ref,
    rate_grad_ref,
    query_in,
    key_in,
    value_in,
    upstream_in,
    residue_in,
    rate_in,
    send_a,
    recv_a,
    send_b,
    recv_b,
    wide,
    xs,
    gs,
    toep_x,
    toep_g,
    end_tables,
    tables,
    in_sems,
    send_sems,
    recv_sems,
):
    blocks_y, blocks_z = sizes
    blocks = blocks_y * blocks_z * 2
    me = lax.axis_index("ctx")
    my_core = lax.rem(me, 2)
    my_z = lax.rem(me // 2, blocks_z)
    my_y = me // (2 * blocks_z)

    half = blocks_z // 2

    def for_far_first(action):
        def hops(offset):
            y, z, _ = offset
            return 2 * min(y, blocks_y - y) + min(z, blocks_z - z)

        ways = [0]
        for z in range(1, half):
            ways += [z, blocks_z - z]
        ways.append(half)
        offsets = [(y, z, core) for z in ways for core in range(2) for y in range(blocks_y)]
        for y, z, core in sorted(offsets[1:], key=hops, reverse=True):
            chip = lax.rem(my_y + y, blocks_y) * blocks_z + lax.rem(my_z + z, blocks_z)
            action(chip * 2 + lax.rem(my_core + core, 2))

    barrier = pltpu.get_barrier_semaphore()

    def greet(peer):
        pl.semaphore_signal(barrier, inc=1, device_id={"ctx": peer}, device_id_type=MESH)

    for_far_first(greet)

    loads = []
    for place, (source, target) in enumerate(
        (
            (key_ref, key_in),
            (value_ref, value_in),
            (query_ref, query_in),
            (upstream_ref, upstream_in),
            (residue_ref, residue_in),
            (rate_ref, rate_in),
        )
    ):
        load = pltpu.make_async_copy(source, target, in_sems.at[place])
        load.start()
        loads.append(load)

    loads[4].wait()
    loads[5].wait()
    rate = rate_in[...]
    residue = residue_in[...]
    spread = (iota((16, LANES), 1) % 16 == iota((16, LANES), 0)).astype(F32)
    own_lane = iota((OWN, LANES), 1) // 16 == iota((OWN, LANES), 0)

    def to_row(params):
        tiled = dot(params, spread, precision=HIGHEST)
        return jnp.sum(jnp.where(own_lane, tiled, 0.0), axis=0, keepdims=True)

    rate_row = to_row(rate)
    gain_row = to_row(residue * jnp.sqrt(rate))

    channels = blocks * OWN
    for array, (left, right) in enumerate(((key_in, value_in), (upstream_in, query_in))):
        loads[2 * array].wait()
        loads[2 * array + 1].wait()
        for first in range(0, channels, LANES):
            cols = pl.ds(first, LANES)
            product = (left[:, cols].astype(F32) * right[:, cols].astype(F32)).astype(BF16)
            send_a[array, pl.ds(first // OWN, LANES // OWN)] = (
                jnp.transpose(product.astype(F32)).reshape(LANES // OWN, OWN, BLOCK).astype(BF16)
            )

    pl.semaphore_wait(barrier, blocks - 1)

    def pusher(send, recv, phase, array):
        def push(peer):
            pltpu.make_async_remote_copy(
                src_ref=send.at[array, peer],
                dst_ref=recv.at[array, me],
                send_sem=send_sems.at[phase, array],
                recv_sem=recv_sems.at[phase, array],
                device_id={"ctx": peer},
                device_id_type=MESH,
            ).start()

        return push

    def keep(send, recv, phase, array):
        pltpu.make_async_copy(
            send.at[array, me], recv.at[array, me], recv_sems.at[phase, array]
        ).start()

    def arrived(recv, phase, array):
        pltpu.make_async_copy(recv.at[array], recv.at[array], recv_sems.at[phase, array]).wait()

    def sent(send, phase, array):
        rest = send.at[array, pl.ds(0, blocks - 1)]
        pltpu.make_async_copy(rest, rest, send_sems.at[phase, array]).wait()

    for array in range(2):
        for_far_first(pusher(send_a, recv_a, 0, array))
        keep(send_a, recv_a, 0, array)
        if array == 0:
            sent(send_a, 0, 0)

    place_row = iota((BLOCK, LANES), 0).astype(F32)
    place_lane = iota((OWN, LANES), 1).astype(F32)
    ahead = jnp.exp(-rate_row * (float(BLOCK - 1) - place_row))
    behind = jnp.exp(-rate_row * (place_row + 1.0))
    for place, table in enumerate((ahead, behind)):
        end_tables[place] = jnp.concatenate(split(table), axis=0)
    for place, table in enumerate((gain_row * behind, gain_row * ahead)):
        high, low = split(table)
        tables[place] = jnp.concatenate([high, high, low], axis=1)
    taps = jnp.zeros((OWN, LANES), F32)
    for mode in range(16):
        mode_rate = rate[:, mode : mode + 1]
        taps = taps + residue[:, mode : mode + 1] * (
            jnp.sqrt(mode_rate) * jnp.exp(-mode_rate * place_lane)
        )
    causal = iota((BLOCK, BLOCK), 1) >= iota((BLOCK, BLOCK), 0)
    for channel in range(OWN):
        row = jnp.broadcast_to(taps[channel : channel + 1], (BLOCK, LANES))
        row = pltpu.roll(row, 0, 1, stride=1, stride_axis=0)
        high, low = split(jnp.where(causal, row, 0.0))
        toep_x[channel] = jnp.concatenate([high, low], axis=0)
        toep_g[channel] = jnp.concatenate([high, low], axis=1)

    group = iota((blocks, LANES), 1) // 16

    def own_signals(array, target):
        arrived(recv_a, 0, array)
        wide[...] = recv_a[array].astype(F32).reshape(blocks * OWN, BLOCK)
        for channel in range(OWN):
            target[pl.ds(channel * blocks, blocks), :] = wide[
                pl.ds(channel, blocks, stride=OWN), :
            ].astype(BF16)
        return target[...]

    def twice(signals):
        return jnp.concatenate([signals, signals], axis=1)

    def respond(array, signals, state, toep, over):
        parts = jnp.concatenate(
            [jnp.where(group == channel, state, 0.0) for channel in range(OWN)], axis=0
        )
        high, low = split(parts)
        carried = dot(jnp.concatenate([high, low, high], axis=1), tables[array], ((1,), (1,)))
        for channel in range(OWN):
            rows = slice(channel * blocks, (channel + 1) * blocks)
            wide[pl.ds(channel, blocks, stride=OWN), :] = (
                dot(twice(signals[rows]), toep[channel], over) + carried[rows]
            )
        send_b[array] = wide[...].reshape(blocks, OWN, BLOCK).astype(BF16)

    x_all = own_signals(0, xs)
    x_ends = own_rows(dot(twice(x_all), end_tables[0]), blocks)
    x_state = scan_blocks(x_ends, rate_row, True)
    respond(0, x_all, x_state, toep_x, ((1,), (0,)))
    for_far_first(pusher(send_b, recv_b, 1, 0))
    keep(send_b, recv_b, 1, 0)

    g_all = own_signals(1, gs)
    g_ends = own_rows(dot(twice(g_all), end_tables[1]), blocks)
    g_state = scan_blocks(g_ends, rate_row, False)
    respond(1, g_all, g_state, toep_g, ((1,), (1,)))
    for_far_first(pusher(send_b, recv_b, 1, 1))
    keep(send_b, recv_b, 1, 1)

    high, low = split(ahead * (float(BLOCK - 1) - place_row))
    x_slopes = own_rows(dot(x_all, high) + dot(x_all, low), blocks)
    high, low = split(behind * (place_row + 1.0))
    g_slopes = own_rows(dot(g_all, high) + dot(g_all, low), blocks)
    x_state, x_moment = scan_moments(x_ends, x_slopes, rate_row)
    plain = jnp.sum(g_ends * x_state, axis=0, keepdims=True)
    sloped = jnp.sum(g_ends * x_moment + g_slopes * x_state, axis=0, keepdims=True)
    reverse = (iota((BLOCK, BLOCK), 0) + iota((BLOCK, BLOCK), 1) == BLOCK - 1).astype(BF16)
    x_reversed = dot(x_all, reverse).astype(BF16)
    paired = iota((BLOCK, BLOCK), 0) + iota((BLOCK, BLOCK), 1) >= BLOCK - 1
    lags = []
    for channel in range(OWN):
        rows = slice(channel * blocks, (channel + 1) * blocks)
        pairs = dot(g_all[rows], x_reversed[rows], ((0,), (0,)))
        pairs = jnp.where(paired, pairs, 0.0)
        pairs = pltpu.roll(pairs, 1, 1, stride=1, stride_axis=0)
        lags.append(jnp.sum(pairs, axis=0, keepdims=True))
    lags = jnp.concatenate(lags, axis=0)
    decays = jnp.exp(-rate_row * place_row)

    def own_sum(table):
        full = dot(lags, table, precision=HIGHEST)
        return jnp.sum(jnp.where(own_lane, full, 0.0), axis=0, keepdims=True)

    plain = plain + own_sum(decays)
    sloped = sloped + own_sum(decays * place_row)
    root_row = jnp.sqrt(rate_row) * scale
    residue_row = to_row(residue)
    gather = (iota((LANES, 16), 0) % 16 == iota((LANES, 16), 1)).astype(F32)

    def from_row(row):
        rows = jnp.where(own_lane, jnp.broadcast_to(row, (OWN, LANES)), 0.0)
        return dot(rows, gather, precision=HIGHEST)

    residue_grad_ref[...] = from_row(root_row * plain)
    rate_grad_ref[...] = from_row(root_row * residue_row * (0.5 * plain - rate_row * sloped))

    products = (
        ((upstream_in, query_grad_ref),),
        ((value_in, key_grad_ref), (key_in, value_grad_ref)),
    )
    for array in range(2):
        arrived(recv_b, 1, array)
        for first in range(0, channels, LANES):
            cols = pl.ds(first, LANES)
            part = recv_b[array, pl.ds(first // OWN, LANES // OWN)].astype(F32)
            part = jnp.transpose(part.reshape(LANES, BLOCK))
            for gate, target in products[array]:
                target[:, cols] = (gate[:, cols].astype(F32) * part).astype(BF16)
    sent(send_a, 0, 1)
    for array in range(2):
        sent(send_b, 1, array)


def finish(*refs):
    count = len(refs) // 2
    sources, targets, sems = refs[:count], refs[count:-1], refs[-1]
    stores = [
        pltpu.make_async_copy(source, target, sems.at[place])
        for place, (source, target) in enumerate(zip(sources, targets))
    ]
    for store in stores:
        store.start()
    for store in stores:
        store.wait()


def local(sizes, query_proj, key_proj, value_proj, output_grad, residue, decay_rate):
    tok_dev, channels = query_proj.shape
    blocks = sizes[0] * sizes[1] * 2
    scale = float(tok_dev * blocks) ** (-0.5)
    anywhere = pl.BlockSpec(memory_space=pl.ANY)
    vmem = pl.BlockSpec(memory_space=pltpu.VMEM)
    tokens = jax.ShapeDtypeStruct((tok_dev, channels), BF16)
    params = jax.ShapeDtypeStruct(residue.shape, F32)
    message = pltpu.VMEM((2, blocks, OWN, BLOCK), BF16)
    tokens_vmem = pltpu.VMEM(tokens.shape, BF16)
    params_vmem = pltpu.VMEM(params.shape, F32)
    results = pl.pallas_call(
        functools.partial(kernel, sizes, scale),
        out_shape=(tokens_vmem,) * 3 + (params_vmem,) * 2,
        in_specs=[anywhere] * 6,
        out_specs=[vmem] * 5,
        scratch_shapes=[pltpu.VMEM((tok_dev, channels), BF16)] * 4
        + [params_vmem] * 2
        + [message] * 4
        + [
            pltpu.VMEM((blocks * OWN, BLOCK), F32),
            pltpu.VMEM((blocks * OWN, BLOCK), BF16),
            pltpu.VMEM((blocks * OWN, BLOCK), BF16),
            pltpu.VMEM((OWN, 2 * BLOCK, BLOCK), BF16),
            pltpu.VMEM((OWN, BLOCK, 2 * BLOCK), BF16),
            pltpu.VMEM((2, 2 * BLOCK, LANES), BF16),
            pltpu.VMEM((2, BLOCK, 3 * LANES), BF16),
            pltpu.SemaphoreType.DMA((6,)),
            pltpu.SemaphoreType.DMA((2, 2)),
            pltpu.SemaphoreType.DMA((2, 2)),
        ],
        compiler_params=pltpu.CompilerParams(collective_id=0, has_side_effects=True, vmem_limit_bytes=60 * 1024 * 1024),
    )(query_proj, key_proj, value_proj, output_grad, residue, decay_rate)
    return pl.pallas_call(
        finish,
        out_shape=(tokens,) * 3 + (params,) * 2,
        in_specs=[vmem] * 5,
        out_specs=[anywhere] * 5,
        scratch_shapes=[pltpu.SemaphoreType.DMA((5,))],
        compiler_params=pltpu.CompilerParams(vmem_limit_bytes=8 << 20),
    )(*results)


def solution(mesh):
    ranks = mesh.shape["ctx"]
    along_z = min(8, ranks // 2)
    sizes = (ranks // (2 * along_z), along_z)
    tokens = P("ctx", "ch")
    params = P(("ch", "ctx"), None)
    return jax.shard_map(
        functools.partial(local, sizes),
        mesh=mesh,
        in_specs=(tokens,) * 4 + (params,) * 2,
        out_specs=(tokens,) * 3 + (params,) * 2,
        check_vma=False,
    )
```

```python
import functools
import math

import jax
import jax.numpy as jnp
from jax import lax
from jax.experimental import pallas as pl
from jax.experimental.pallas import tpu as pltpu
from jax.sharding import PartitionSpec as P

MESH = pl.DeviceIdType.MESH
F32 = jnp.float32
BF16 = jnp.bfloat16
HIGHEST = lax.Precision.HIGHEST
BLOCK = 128
OWN = 8
LANES = 128


def dot(left, right, dims=((1,), (0,)), precision=None):
    return lax.dot_general(
        left, right, (dims, ((), ())), precision=precision, preferred_element_type=F32
    )


def split(value):
    high = value.astype(BF16)
    return high, (value - high.astype(F32)).astype(BF16)


def iota(shape, axis):
    return lax.broadcasted_iota(jnp.int32, shape, axis)


def shift_rows(value, step, down):
    rows = value.shape[0]
    index = iota(value.shape, 0)
    if down:
        return jnp.where(index >= step, pltpu.roll(value, step, 0), 0.0)
    return jnp.where(index < rows - step, pltpu.roll(value, rows - step, 0), 0.0)


def scan_blocks(state, rate_row, down):
    step = 1
    while step < state.shape[0]:
        decay = jnp.exp(rate_row * (-float(BLOCK * step)))
        state = state + decay * shift_rows(state, step, down)
        step *= 2
    return shift_rows(state, 1, down)


def scan_moments(state, moment, rate_row):
    step = 1
    while step < state.shape[0]:
        decay = jnp.exp(rate_row * (-float(BLOCK * step)))
        below = shift_rows(state, step, True)
        moment = moment + decay * (
            shift_rows(moment, step, True) + float(BLOCK * step) * below
        )
        state = state + decay * below
        step *= 2
    return shift_rows(state, 1, True), shift_rows(moment, 1, True)


def own_rows(stacked, blocks):
    group = iota((blocks, LANES), 1) // 16
    total = jnp.zeros((blocks, LANES), F32)
    for channel in range(OWN):
        part = stacked[channel * blocks : (channel + 1) * blocks]
        total = jnp.where(group == channel, part, total)
    return total


def kernel(
    sizes,
    scale,
    query_ref,
    key_ref,
    value_ref,
    upstream_ref,
    residue_ref,
    rate_ref,
    query_grad_ref,
    key_grad_ref,
    value_grad_ref,
    residue_grad_ref,
    rate_grad_ref,
    query_in,
    key_in,
    value_in,
    upstream_in,
    residue_in,
    rate_in,
    send_a,
    recv_a,
    send_b,
    recv_b,
    wide,
    toep_x,
    toep_g,
    end_tables,
    tables,
    in_sems,
    send_sems,
    recv_sems,
):
    blocks_y, blocks_z = sizes
    blocks = blocks_y * blocks_z * 2
    me = lax.axis_index("ctx")
    my_core = lax.rem(me, 2)
    my_z = lax.rem(me // 2, blocks_z)
    my_y = me // (2 * blocks_z)

    half = blocks_z // 2

    def for_far_first(action):
        def hops(offset):
            y, z, _ = offset
            return 2 * min(y, blocks_y - y) + min(z, blocks_z - z)

        ways = [0]
        for z in range(1, half):
            ways += [z, blocks_z - z]
        ways.append(half)
        offsets = [(y, z, core) for z in ways for core in range(2) for y in range(blocks_y)]
        for y, z, core in sorted(offsets[1:], key=hops, reverse=True):
            chip = lax.rem(my_y + y, blocks_y) * blocks_z + lax.rem(my_z + z, blocks_z)
            action(chip * 2 + lax.rem(my_core + core, 2))

    barrier = pltpu.get_barrier_semaphore()

    def greet(peer):
        pl.semaphore_signal(barrier, inc=1, device_id={"ctx": peer}, device_id_type=MESH)

    for_far_first(greet)

    loads = []
    for place, (source, target) in enumerate(
        (
            (key_ref, key_in),
            (value_ref, value_in),
            (query_ref, query_in),
            (upstream_ref, upstream_in),
            (residue_ref, residue_in),
            (rate_ref, rate_in),
        )
    ):
        load = pltpu.make_async_copy(source, target, in_sems.at[place])
        load.start()
        loads.append(load)

    loads[4].wait()
    loads[5].wait()
    rate = rate_in[...]
    residue = residue_in[...]
    spread = (iota((16, LANES), 1) % 16 == iota((16, LANES), 0)).astype(F32)
    own_lane = iota((OWN, LANES), 1) // 16 == iota((OWN, LANES), 0)

    def to_row(params):
        tiled = dot(params, spread, precision=HIGHEST)
        return jnp.sum(jnp.where(own_lane, tiled, 0.0), axis=0, keepdims=True)

    rate_row = to_row(rate)
    gain_row = to_row(residue * jnp.sqrt(rate))

    channels = blocks * OWN
    for array, (left, right) in enumerate(((key_in, value_in), (upstream_in, query_in))):
        loads[2 * array].wait()
        loads[2 * array + 1].wait()
        for first in range(0, channels, LANES):
            cols = pl.ds(first, LANES)
            product = (left[:, cols].astype(F32) * right[:, cols].astype(F32)).astype(BF16)
            send_a[array, pl.ds(first // OWN, LANES // OWN)] = (
                jnp.transpose(product.astype(F32)).reshape(LANES // OWN, OWN, BLOCK).astype(BF16)
            )

    pl.semaphore_wait(barrier, blocks - 1)

    def pusher(send, recv, phase, array):
        def push(peer):
            pltpu.make_async_remote_copy(
                src_ref=send.at[array, peer],
                dst_ref=recv.at[array, me],
                send_sem=send_sems.at[phase, array],
                recv_sem=recv_sems.at[phase, array],
                device_id={"ctx": peer},
                device_id_type=MESH,
            ).start()

        return push

    def keep(send, recv, phase, array):
        pltpu.make_async_copy(
            send.at[array, me], recv.at[array, me], recv_sems.at[phase, array]
        ).start()

    def arrived(recv, phase, array):
        pltpu.make_async_copy(recv.at[array], recv.at[array], recv_sems.at[phase, array]).wait()

    def sent(send, phase, array):
        rest = send.at[array, pl.ds(0, blocks - 1)]
        pltpu.make_async_copy(rest, rest, send_sems.at[phase, array]).wait()

    for array in range(2):
        for_far_first(pusher(send_a, recv_a, 0, array))
        keep(send_a, recv_a, 0, array)
        if array == 0:
            sent(send_a, 0, 0)

    place_row = iota((BLOCK, LANES), 0).astype(F32)
    place_lane = iota((OWN, LANES), 1).astype(F32)
    ahead = jnp.exp(-rate_row * (float(BLOCK - 1) - place_row))
    behind = jnp.exp(-rate_row * (place_row + 1.0))
    for place, table in enumerate((ahead, behind)):
        end_tables[place] = jnp.concatenate(split(table), axis=0)
    for place, table in enumerate((gain_row * behind, gain_row * ahead)):
        high, low = split(table)
        tables[place] = jnp.concatenate([high, high, low], axis=1)
    taps = jnp.zeros((OWN, LANES), F32)
    for mode in range(16):
        mode_rate = rate[:, mode : mode + 1]
        taps = taps + residue[:, mode : mode + 1] * (
            jnp.sqrt(mode_rate) * jnp.exp(-mode_rate * place_lane)
        )
    causal = iota((BLOCK, BLOCK), 1) >= iota((BLOCK, BLOCK), 0)
    for channel in range(OWN):
        row = jnp.broadcast_to(taps[channel : channel + 1], (BLOCK, LANES))
        row = pltpu.roll(row, 0, 1, stride=1, stride_axis=0)
        high, low = split(jnp.where(causal, row, 0.0))
        toep_x[channel] = jnp.concatenate([high, low], axis=0)
        toep_g[channel] = jnp.concatenate([high, low], axis=1)

    group = iota((blocks, LANES), 1) // 16

    def own_signals(array):
        arrived(recv_a, 0, array)
        wide[...] = recv_a[array].astype(F32).reshape(blocks * OWN, BLOCK)
        return jnp.concatenate(
            [wide[pl.ds(channel, blocks, stride=OWN), :].astype(BF16) for channel in range(OWN)],
            axis=0,
        )

    def twice(signals):
        return jnp.concatenate([signals, signals], axis=1)

    def respond(array, signals, state, toep, over):
        parts = jnp.concatenate(
            [jnp.where(group == channel, state, 0.0) for channel in range(OWN)], axis=0
        )
        high, low = split(parts)
        carried = dot(jnp.concatenate([high, low, high], axis=1), tables[array], ((1,), (1,)))
        for channel in range(OWN):
            rows = slice(channel * blocks, (channel + 1) * blocks)
            wide[pl.ds(channel, blocks, stride=OWN), :] = (
                dot(twice(signals[rows]), toep[channel], over) + carried[rows]
            )
        send_b[array] = wide[...].reshape(blocks, OWN, BLOCK).astype(BF16)

    x_all = own_signals(0)
    x_ends = own_rows(dot(twice(x_all), end_tables[0]), blocks)
    x_state = scan_blocks(x_ends, rate_row, True)
    respond(0, x_all, x_state, toep_x, ((1,), (0,)))
    for_far_first(pusher(send_b, recv_b, 1, 0))
    keep(send_b, recv_b, 1, 0)

    g_all = own_signals(1)
    g_ends = own_rows(dot(twice(g_all), end_tables[1]), blocks)
    g_state = scan_blocks(g_ends, rate_row, False)
    respond(1, g_all, g_state, toep_g, ((1,), (1,)))
    for_far_first(pusher(send_b, recv_b, 1, 1))
    keep(send_b, recv_b, 1, 1)

    high, low = split(ahead * (float(BLOCK - 1) - place_row))
    x_slopes = own_rows(dot(x_all, high) + dot(x_all, low), blocks)
    high, low = split(behind * (place_row + 1.0))
    g_slopes = own_rows(dot(g_all, high) + dot(g_all, low), blocks)
    x_state, x_moment = scan_moments(x_ends, x_slopes, rate_row)
    plain = jnp.sum(g_ends * x_state, axis=0, keepdims=True)
    sloped = jnp.sum(g_ends * x_moment + g_slopes * x_state, axis=0, keepdims=True)
    reverse = (iota((BLOCK, BLOCK), 0) + iota((BLOCK, BLOCK), 1) == BLOCK - 1).astype(BF16)
    x_reversed = dot(x_all, reverse).astype(BF16)
    paired = iota((BLOCK, BLOCK), 0) + iota((BLOCK, BLOCK), 1) >= BLOCK - 1
    lags = []
    for channel in range(OWN):
        rows = slice(channel * blocks, (channel + 1) * blocks)
        pairs = dot(g_all[rows], x_reversed[rows], ((0,), (0,)))
        pairs = jnp.where(paired, pairs, 0.0)
        pairs = pltpu.roll(pairs, 1, 1, stride=1, stride_axis=0)
        lags.append(jnp.sum(pairs, axis=0, keepdims=True))
    lags = jnp.concatenate(lags, axis=0)
    decays = jnp.exp(-rate_row * place_row)

    def own_sum(table):
        full = dot(lags, table, precision=HIGHEST)
        return jnp.sum(jnp.where(own_lane, full, 0.0), axis=0, keepdims=True)

    plain = plain + own_sum(decays)
    sloped = sloped + own_sum(decays * place_row)
    root_row = jnp.sqrt(rate_row) * scale
    residue_row = to_row(residue)
    gather = (iota((LANES, 16), 0) % 16 == iota((LANES, 16), 1)).astype(F32)

    def from_row(row):
        rows = jnp.where(own_lane, jnp.broadcast_to(row, (OWN, LANES)), 0.0)
        return dot(rows, gather, precision=HIGHEST)

    residue_grad_ref[...] = from_row(root_row * plain)
    rate_grad_ref[...] = from_row(root_row * residue_row * (0.5 * plain - rate_row * sloped))

    products = (
        ((upstream_in, query_grad_ref),),
        ((value_in, key_grad_ref), (key_in, value_grad_ref)),
    )
    for array in range(2):
        arrived(recv_b, 1, array)
        for first in range(0, channels, LANES):
            cols = pl.ds(first, LANES)
            part = recv_b[array, pl.ds(first // OWN, LANES // OWN)].astype(F32)
            part = jnp.transpose(part.reshape(LANES, BLOCK))
            for gate, target in products[array]:
                target[:, cols] = (gate[:, cols].astype(F32) * part).astype(BF16)
    sent(send_a, 0, 1)
    for array in range(2):
        sent(send_b, 1, array)


def finish(*refs):
    count = len(refs) // 2
    sources, targets, sems = refs[:count], refs[count:-1], refs[-1]
    stores = [
        pltpu.make_async_copy(source, target, sems.at[place])
        for place, (source, target) in enumerate(zip(sources, targets))
    ]
    for store in stores:
        store.start()
    for store in stores:
        store.wait()


def local(sizes, query_proj, key_proj, value_proj, output_grad, residue, decay_rate):
    tok_dev, channels = query_proj.shape
    blocks = sizes[0] * sizes[1] * 2
    scale = float(tok_dev * blocks) ** (-0.5)
    anywhere = pl.BlockSpec(memory_space=pl.ANY)
    vmem = pl.BlockSpec(memory_space=pltpu.VMEM)
    tokens = jax.ShapeDtypeStruct((tok_dev, channels), BF16)
    params = jax.ShapeDtypeStruct(residue.shape, F32)
    message = pltpu.VMEM((2, blocks, OWN, BLOCK), BF16)
    tokens_vmem = pltpu.VMEM(tokens.shape, BF16)
    params_vmem = pltpu.VMEM(params.shape, F32)
    results = pl.pallas_call(
        functools.partial(kernel, sizes, scale),
        out_shape=(tokens_vmem,) * 3 + (params_vmem,) * 2,
        in_specs=[anywhere] * 6,
        out_specs=[vmem] * 5,
        scratch_shapes=[pltpu.VMEM((tok_dev, channels), BF16)] * 4
        + [params_vmem] * 2
        + [message] * 4
        + [
            pltpu.VMEM((blocks * OWN, BLOCK), F32),
            pltpu.VMEM((OWN, 2 * BLOCK, BLOCK), BF16),
            pltpu.VMEM((OWN, BLOCK, 2 * BLOCK), BF16),
            pltpu.VMEM((2, 2 * BLOCK, LANES), BF16),
            pltpu.VMEM((2, BLOCK, 3 * LANES), BF16),
            pltpu.SemaphoreType.DMA((6,)),
            pltpu.SemaphoreType.DMA((2, 2)),
            pltpu.SemaphoreType.DMA((2, 2)),
        ],
        compiler_params=pltpu.CompilerParams(collective_id=0, has_side_effects=True, vmem_limit_bytes=60 * 1024 * 1024),
    )(query_proj, key_proj, value_proj, output_grad, residue, decay_rate)
    return pl.pallas_call(
        finish,
        out_shape=(tokens,) * 3 + (params,) * 2,
        in_specs=[vmem] * 5,
        out_specs=[anywhere] * 5,
        scratch_shapes=[pltpu.SemaphoreType.DMA((5,))],
        compiler_params=pltpu.CompilerParams(vmem_limit_bytes=8 << 20),
    )(*results)


def solution(mesh):
    ranks = mesh.shape["ctx"]
    along_z = min(8, ranks // 2)
    sizes = (ranks // (2 * along_z), along_z)
    tokens = P("ctx", "ch")
    params = P(("ch", "ctx"), None)
    return jax.shard_map(
        functools.partial(local, sizes),
        mesh=mesh,
        in_specs=(tokens,) * 4 + (params,) * 2,
        out_specs=(tokens,) * 3 + (params,) * 2,
        check_vma=False,
    )
```
